512 devices in a mesh: lat: 64 (over z, y), rad: 8 (over x, core).
Axes of the slice: x: 4, y: 8, z: 8, core: 2. Of those that a mesh axis runs over, the one named last changes fastest.
Arguments:
- tracer_values: float32 [64, 8, 3, 49152], P('lat', 'rad'), may hold values from 0 to 1
- tracer_cell: int32 [64, 8, 49152], P('lat', 'rad'), may hold values from 0 to 18431, as said below
- tracer_count: int32 [64, 8, 3], P('lat', 'rad'), may hold values from 2048 to 16384, as said below
- base_viscosity: float32 [768, 96, 128], P('lat', 'rad'), may hold values from 0.3 to 3
- velocity: float32 [3, 768, 96, 128], P(None, 'lat', 'rad'), may hold values from -6 to 6
- forcing: float32 [3, 768, 96, 128], P(None, 'lat', 'rad'), may hold values from -4 to 4
Outputs:
- smoothed: float32 [3, 768, 96, 128], P(None, 'lat', 'rad')
- composition: float32 [2, 768, 96, 128], P(None, 'lat', 'rad')
The draws below stay inside these ranges and needn't reach their ends.
Inputs may be any that keep to these rules, and one draw needn't show every extreme that they name: `tracer_count`: in group g of a device (0: going to the device one lower along lat, 1: staying, 2: going to the device one higher) slots 0 to count - 1 hold tracers and the rest are empty; for every group some device has all 16384 slots in use (used slots, live or not). `tracer_cell`: index ((x * 12) + r) * 128 + y of a cell in the block of the device the tracer goes to, at the same rad index; tracers of slots below 16384 land in the last 2 x-planes of their device, tracers of slots from 32768 on in the first 2 x-planes.
All inputs are finite; a program needn't handle non-finite values.
Results may differ from the reference program's by a relative error of at most 0.0003.
The reference program's roundings to bfloat16 on the way (of `tracer_loads`) count: a program that leaves them out, or rounds other values in their place, can miss the bound.
Values sent between devices are 32-bit elements; how exact they have to be, the bound alone decides.
A program may use at most 64 MiB of HBM per device.

```python
import math
import jax
import jax.numpy as jnp
from jax import lax

CX = 12
CR = 12
NY = 128
CAP = 16384
MIG = 2
SWEEPS = 2
LAT_DEVICES = 64
RAD_DEVICES = 8
NX = 768
NR = 96
SLOTS = 49152


def draw_tracer_cell(key, part):
    key_any, key_lower, key_upper, key_radial, key_side = jax.random.split(key, 5)
    array_shape = (LAT_DEVICES, RAD_DEVICES, 3 * CAP)
    slot_index = lax.broadcasted_iota(jnp.int32, array_shape, 2)
    group_index = slot_index // CAP
    plane_any = jax.random.randint(key_any, array_shape, 0, CX)
    plane_lower = jax.random.randint(key_lower, array_shape, CX - MIG, CX)
    plane_upper = jax.random.randint(key_upper, array_shape, 0, MIG)
    plane_index = jnp.where(group_index == 0, plane_lower, jnp.where(group_index == 2, plane_upper, plane_any))
    radial_index = jax.random.randint(key_radial, array_shape, 0, CR)
    side_index = jax.random.randint(key_side, array_shape, 0, NY)
    return ((plane_index * CR + radial_index) * NY + side_index).astype(jnp.int32)


def draw_tracer_count(key, part):
    key_base, key_heavy, key_band, key_full = jax.random.split(key, 4)
    count_shape = (LAT_DEVICES, RAD_DEVICES, 3)
    regular = jax.random.randint(key_base, count_shape, CAP // 8, CAP // 2 + 1)
    heavy_count = jax.random.randint(key_heavy, count_shape, 3 * CAP // 4, CAP + 1)
    band_start = jax.random.randint(key_band, (), 0, LAT_DEVICES)
    lateral = lax.broadcasted_iota(jnp.int32, count_shape, 0)
    in_band = (lateral - band_start) % LAT_DEVICES < max(1, LAT_DEVICES // 8)
    counts = jnp.where(in_band, heavy_count, regular)
    radial_full = jax.random.randint(key_full, (), 0, RAD_DEVICES)
    counts = counts.at[band_start, radial_full, :].set(CAP)
    light_device = (band_start + LAT_DEVICES // 2) % LAT_DEVICES
    counts = counts.at[light_device, 0, 0].set(CAP // 8)
    return counts.astype(jnp.int32)


def draw_forcing(key, part):
    key_noise = jax.random.fold_in(key, 0)
    field_shape = (3, NX, NR, NY)
    noise = jax.random.normal(key_noise, field_shape, jnp.float32)
    return jnp.clip(0.5 * noise, -4.0, 4.0).astype(jnp.float32)


def level_of(rng, extent, pieces, least, top_value):
    level, own = 1.0, jax.random.fold_in(rng, 6)
    for dim, blocks in pieces:
        steps = jnp.exp(jax.random.uniform(jax.random.fold_in(own, dim), (blocks,), jnp.float32, least / len(pieces), top_value / len(pieces)))
        level = level * jnp.repeat(steps, extent[dim] // blocks).reshape([-1 if axis == dim else 1 for axis in range(len(extent))])
    return level


def bell_draw(rng, dims, scale, limit, pieces=(), dtype=jnp.bfloat16):
    array = jax.random.normal(rng, dims, jnp.float32) * scale
    if len(pieces) > 0:
        array = level_of(rng, dims, pieces, -0.22, 0.18) * array
    return jnp.clip(array, min=-limit, max=limit).astype(dtype)


def setup_inputs(seed: int = 0) -> dict:
    key_of = jax.random.split(jax.random.key(seed), 7)
    tracer_values = jnp.clip(1.0 * jax.random.uniform(key_of[0], (LAT_DEVICES, RAD_DEVICES, 3, SLOTS), jnp.float32) ** level_of(key_of[0], (LAT_DEVICES, RAD_DEVICES, 3, SLOTS), ((0, 64), (1, 8)), -0.2, 0.2), 0.0, 1.0)
    tracer_cell = draw_tracer_cell(jax.random.fold_in(key_of[6], 71), 0)
    tracer_count = draw_tracer_count(jax.random.fold_in(key_of[6], 71), 0)
    base_viscosity = jnp.clip(jnp.exp(math.log(3.0) - 2.3025851 * jax.random.uniform(key_of[3], (NX, NR, NY), jnp.float32) ** level_of(key_of[3], (NX, NR, NY), ((0, 64), (1, 8)), -0.2, 0.2)), 0.3, 3.0)
    velocity = bell_draw(key_of[4], (3, NX, NR, NY), 1.0, 6.0, ((1, 64), (2, 8)), jnp.float32)
    forcing = draw_forcing(jax.random.fold_in(key_of[6], 71), 0)
    return {"tracer_values": tracer_values, "tracer_cell": tracer_cell, "tracer_count": tracer_count, "base_viscosity": base_viscosity, "velocity": velocity, "forcing": forcing}


LATERAL = 0.015625
RADIAL = 32.0
BUOYANCY = 0.1
PRIOR_WEIGHT = 0.5
CONTRAST_BASALT = 2.3
CONTRAST_MELT = 1.5


def face_terms(viscosity):
    padded = jnp.pad(viscosity, 1)
    face_west = LATERAL * 0.5 * (viscosity + padded[:-2, 1:-1, 1:-1])
    face_east = LATERAL * 0.5 * (viscosity + padded[2:, 1:-1, 1:-1])
    face_south = LATERAL * 0.5 * (viscosity + padded[1:-1, 1:-1, :-2])
    face_north = LATERAL * 0.5 * (viscosity + padded[1:-1, 1:-1, 2:])
    face_below = RADIAL * 0.5 * (viscosity + padded[1:-1, :-2, 1:-1])
    face_above = RADIAL * 0.5 * (viscosity + padded[1:-1, 2:, 1:-1])
    return face_west, face_east, face_south, face_north, face_below, face_above


def line_solve(diagonal, lower_band, upper_band, right_side):
    diag_rows = jnp.moveaxis(diagonal, 1, 0)
    lower_rows = jnp.moveaxis(lower_band, 1, 0)
    upper_rows = jnp.moveaxis(upper_band, 1, 0)
    right_rows = jnp.moveaxis(right_side, 2, 0)

    def forward(carried, inputs):
        upper_prev, right_prev = carried
        diag_row, lower_row, upper_row, right_row = inputs
        pivot_row = diag_row - lower_row * upper_prev
        upper_next = upper_row / pivot_row
        right_next = (right_row - lower_row * right_prev) / pivot_row
        return (upper_next, right_next), (upper_next, right_next)

    start_state = (jnp.zeros((NX, NY), jnp.float32), jnp.zeros((3, NX, NY), jnp.float32))
    final_state, eliminated = lax.scan(forward, start_state, (diag_rows, lower_rows, upper_rows, right_rows))

    def backward(solved_next, inputs):
        upper_row, right_row = inputs
        solved = right_row - upper_row * solved_next
        return solved, solved

    final_value, solved_rows = lax.scan(backward, jnp.zeros((3, NX, NY), jnp.float32), eliminated, reverse=True)
    return jnp.moveaxis(solved_rows, 0, 2)


def reference(tracer_values, tracer_cell, tracer_count, base_viscosity, velocity, forcing):
    grid_shape = (LAT_DEVICES, RAD_DEVICES, SLOTS)
    slot_index = lax.broadcasted_iota(jnp.int32, grid_shape, 2)
    lateral = lax.broadcasted_iota(jnp.int32, grid_shape, 0)
    radial = lax.broadcasted_iota(jnp.int32, grid_shape, 1)
    group_index = slot_index // CAP
    within = slot_index - group_index * CAP
    count_slot = jnp.take_along_axis(tracer_count, group_index, axis=2)
    target = lateral + group_index - 1
    is_valid = (within < count_slot) & (target >= 0) & (target < LAT_DEVICES)
    weight = jnp.where(is_valid, 0.5 + tracer_values[:, :, 0, :], jnp.float32(0.0))
    rounded = jnp.stack([weight, weight * tracer_values[:, :, 1, :], weight * tracer_values[:, :, 2, :]]).astype(jnp.bfloat16)
    rounded = lax.optimization_barrier(rounded)
    tracer_loads = rounded.astype(jnp.float32)
    column_x = jnp.clip(target, 0, LAT_DEVICES - 1) * CX + tracer_cell // (CR * NY)
    column_r = radial * CR + (tracer_cell // NY) % CR
    column_y = tracer_cell % NY
    flat_cell = ((column_x * NR + column_r) * NY + column_y).astype(jnp.int32).reshape(-1)
    cell_sums = jax.ops.segment_sum(tracer_loads.reshape(3, -1).T, flat_cell, num_segments=NX * NR * NY)
    cell_sums = cell_sums.T.reshape(3, NX, NR, NY)
    total_weight = cell_sums[0] + PRIOR_WEIGHT
    basalt_share = cell_sums[1] / total_weight
    melt_share = cell_sums[2] / total_weight
    viscosity = base_viscosity * jnp.exp(CONTRAST_BASALT * basalt_share - CONTRAST_MELT * melt_share)
    face_west, face_east, face_south, face_north, face_below, face_above = face_terms(viscosity)
    diagonal = face_west + face_east + face_south + face_north + face_below + face_above
    source = jnp.concatenate([forcing[:2], (forcing[2] - BUOYANCY * basalt_share)[None]], 0)
    radial_index = lax.broadcasted_iota(jnp.int32, (NX, NR, NY), 1)
    lower_band = -face_below
    upper_band = jnp.where(radial_index < NR - 1, -face_above, jnp.float32(0.0))
    current = velocity
    for sweep_index in range(SWEEPS):
        padded = jnp.pad(current, ((0, 0), (1, 1), (0, 0), (1, 1)))
        right_side = source + face_west * padded[:, :-2, :, 1:-1] + face_east * padded[:, 2:, :, 1:-1] + face_south * padded[:, 1:-1, :, :-2] + face_north * padded[:, 1:-1, :, 2:]
        current = line_solve(diagonal, lower_band, upper_band, right_side)
    composition = jnp.stack([basalt_share, melt_share])
    return current, composition
```

```python
import functools

import jax
import jax.numpy as jnp
from jax import lax
from jax.experimental import pallas as pl
from jax.experimental.pallas import tpu as pltpu
from jax.sharding import PartitionSpec as P

MESH = pl.DeviceIdType.MESH
F32 = jnp.float32
BF16 = jnp.bfloat16

SWEEPS = 2
LATERAL = 0.015625
RADIAL = 32.0
BUOYANCY = 0.1
PRIOR_WEIGHT = 0.5
CONTRAST_BASALT = 2.3
CONTRAST_MELT = 1.5

SLOTS = 16
HALO = 2
LANES = 128
Q1 = 24
Q2 = 16


def side_index(cell, first_plane, cr):
    rows = (cell >> 7) - first_plane * cr
    plane = (rows >= cr).astype(jnp.int32)
    radial = rows - cr * plane
    return (plane * 2 + (radial & 1)) * 8 + (radial >> 1)


def stay_index(cell, cr):
    rows = cell >> 8
    half = cr // 2
    plane = (rows * 43691) >> 18
    return (rows - half * plane) * SLOTS + plane + HALO


def hot_masks(index, tiles):
    base = lax.broadcasted_iota(jnp.int32, (16, LANES), 0).astype(F32)
    return [index == (base + 16.0 * t).astype(BF16) for t in range(tiles)]


def bin_group(acc, loads, index_a, index_b, first_row, rows, step_rows, tiles_a, tiles_b, total_rows):
    zero = jnp.zeros((16, LANES), BF16)
    one = jnp.ones((16, LANES), BF16)

    def spread(ref, row):
        return jnp.broadcast_to(ref[pl.ds(row, 1), :], (16, LANES)).astype(BF16)

    def body(step, carry):
        left, right = [], []
        for j in range(step_rows):
            row = first_row + step * step_rows + j
            values = [spread(loads, q * total_rows + row) for q in range(3)]
            hot_a = hot_masks(spread(index_a, row), tiles_a)
            hot_b = hot_masks(spread(index_b, row), tiles_b)
            left.append(jnp.concatenate([jnp.where(h, v, zero) for v in values for h in hot_a], 0))
            right.append(jnp.concatenate([jnp.where(h, one, zero) for h in hot_b], 0))
        acc[...] += lax.dot_general(
            jnp.concatenate(left, 1),
            jnp.concatenate(right, 1),
            (((1,), (1,)), ((), ())),
            preferred_element_type=F32,
        )
        return carry

    lax.fori_loop(0, rows // step_rows, body, 0)


def kernel(
    nl, nk, vals, cell, cnt, bv, vel, frc, out, comp,
    loads, index_a, index_b, acc_s, acc_0, acc_2, edge_lo, edge_hi, got_a_lo, got_a_hi, got_b_lo, got_b_hi,
    hv_lo, hv_hi, hf_lo, hf_hi, hb_lo, hb_hi,
    ext, vs, fs, bs, visc, f_w, f_e, f_s, f_n, up, ip, res0, res1, part,
    snd1, rcv1, bck1, ans1, snd2, rcv2, bck2, ans2,
    lat_send, lat_recv, rad_send, rad_recv,
):
    cx, cr = bv.shape[0], bv.shape[1]
    total_rows = cell.shape[0]
    rows = total_rows // 3
    l = lax.axis_index("lat")
    k = lax.axis_index("rad")
    lm = lax.rem(l + nl - 1, nl)
    lp = lax.rem(l + 1, nl)
    first_l, last_l = l == 0, l == nl - 1

    barrier = pltpu.get_barrier_semaphore()
    for other in (lm, lp):
        pl.semaphore_signal(barrier, inc=1, device_id=(other, k), device_id_type=MESH)
    for d in range(1, nk):
        pl.semaphore_signal(barrier, inc=1, device_id=(l, lax.rem(k + d, nk)), device_id_type=MESH)

    def to_lat(src, dst, other, n):
        return pltpu.make_async_remote_copy(
            src_ref=src, dst_ref=dst, send_sem=lat_send.at[n], recv_sem=lat_recv.at[n],
            device_id=(other, k), device_id_type=MESH,
        )

    place = lax.broadcasted_iota(jnp.int32, (rows, LANES), 0) * LANES + lax.broadcasted_iota(
        jnp.int32, (rows, LANES), 1
    )
    for g in (0, 2, 1):
        sl = pl.ds(g * rows, rows)
        weight = jnp.where(place < cnt[0, 0, g], 0.5 + vals[sl, :], 0.0)
        loads[sl, :] = weight
        loads[pl.ds(total_rows + g * rows, rows), :] = weight * vals[pl.ds(total_rows + g * rows, rows), :]
        loads[pl.ds(2 * total_rows + g * rows, rows), :] = weight * vals[pl.ds(2 * total_rows + g * rows, rows), :]
        c = cell[sl, :]
        if g == 1:
            index_a[sl, :] = stay_index(c, cr).astype(F32)
            index_b[sl, :] = (c & 255).astype(F32)
        else:
            index_a[sl, :] = side_index(c, cx - HALO if g == 0 else 0, cr).astype(F32)
            index_b[sl, :] = (c & 127).astype(F32)

    step_rows = min(32, rows)
    acc_0[...] = jnp.zeros_like(acc_0)
    acc_2[...] = jnp.zeros_like(acc_2)
    acc_s[...] = jnp.zeros_like(acc_s)
    bin_group(acc_0, loads, index_a, index_b, 0, rows, step_rows, 2, 8, total_rows)
    bin_group(acc_2, loads, index_a, index_b, 2 * rows, rows, step_rows, 2, 8, total_rows)

    pl.semaphore_wait(barrier, nk + 1)
    early = [
        to_lat(acc_0, got_a_hi, lm, 0),
        to_lat(acc_2, got_a_lo, lp, 1),
        to_lat(vel.at[:, pl.ds(0, HALO)], hv_hi, lm, 2),
        to_lat(vel.at[:, pl.ds(cx - HALO, HALO)], hv_lo, lp, 3),
        to_lat(frc.at[:, pl.ds(0, 1)], hf_hi, lm, 4),
        to_lat(frc.at[:, pl.ds(cx - 1, 1)], hf_lo, lp, 5),
        to_lat(bv.at[pl.ds(0, HALO)], hb_hi, lm, 6),
        to_lat(bv.at[pl.ds(cx - HALO, HALO)], hb_lo, lp, 7),
    ]
    for copy in early:
        copy.start()

    bin_group(acc_s, loads, index_a, index_b, rows, rows, step_rows, 6, 16, total_rows)

    half = cr // 2
    for q in range(3):
        for h in range(2):
            for s in range(HALO):
                row = q * 32 + (s * 2 + h) * 8
                lanes = pl.ds(h * LANES, LANES)
                edge_lo[pl.ds(row, 8), :] = jnp.zeros((8, LANES), F32)
                edge_hi[pl.ds(row, 8), :] = jnp.zeros((8, LANES), F32)
                for p in range(half):
                    base = q * half * SLOTS + p * SLOTS
                    edge_lo[pl.ds(row + p, 1), :] = acc_s[pl.ds(base + HALO + s, 1), lanes]
                    edge_hi[pl.ds(row + p, 1), :] = acc_s[pl.ds(base + HALO + cx - HALO + s, 1), lanes]
    late = [to_lat(edge_lo, got_b_hi, lm, 8), to_lat(edge_hi, got_b_lo, lp, 9)]
    for copy in late:
        copy.start()

    def put(dst, base, slot, value):
        dst[pl.ds(base + slot, cr, stride=SLOTS), :] = value

    keep_lo = jnp.where(first_l, 0.0, 1.0)
    keep_hi = jnp.where(last_l, 0.0, 1.0)
    zeros = jnp.zeros((cr, LANES), F32)
    for x in range(cx):
        put(bs, 0, x + HALO, bv[x])
        for c in range(3):
            put(vs, c * cr * SLOTS, x + HALO, vel[c, x])
            put(fs, c * cr * SLOTS, x + HALO, frc[c, x])
    for c in range(3):
        put(fs, c * cr * SLOTS, 0, zeros)
        put(fs, c * cr * SLOTS, SLOTS - 1, zeros)
    ext[...] = jnp.zeros_like(ext)
    for copy in early[2:]:
        copy.wait_recv()
    for s in range(HALO):
        put(bs, 0, s, hb_lo[s])
        put(bs, 0, SLOTS - HALO + s, hb_hi[s])
        for c in range(3):
            put(vs, c * cr * SLOTS, s, hv_lo[c, s] * keep_lo)
            put(vs, c * cr * SLOTS, SLOTS - HALO + s, hv_hi[c, s] * keep_hi)
    for c in range(3):
        put(fs, c * cr * SLOTS, HALO - 1, hf_lo[c, 0])
        put(fs, c * cr * SLOTS, SLOTS - HALO, hf_hi[c, 0])

    def put_edge(ref, slot, scale):
        for q in range(3):
            for h in range(2):
                for s in range(HALO):
                    value = ref[pl.ds(q * 32 + (s * 2 + h) * 8, half), :] * scale
                    ext[pl.ds(q * cr * SLOTS + h * SLOTS + slot + s, half, stride=2 * SLOTS), :] = value

    early[0].wait_recv()
    early[1].wait_recv()
    put_edge(got_a_lo, HALO, keep_lo)
    put_edge(got_a_hi, SLOTS - 2 * HALO, keep_hi)
    for copy in late:
        copy.wait_recv()
    got_b_lo[...] += acc_0[...]
    got_b_hi[...] += acc_2[...]
    put_edge(got_b_lo, 0, 1.0)
    put_edge(got_b_hi, SLOTS - HALO, 1.0)

    slot = lax.broadcasted_iota(jnp.int32, (SLOTS, LANES), 0)
    lane = lax.broadcasted_iota(jnp.int32, (SLOTS, LANES), 1)
    low = jnp.where(first_l, HALO, 0)
    high = jnp.where(last_l, SLOTS - HALO, SLOTS)
    inside = jnp.where((slot >= low) & (slot < high), 1.0, 0.0)
    is_west = lane == 0
    is_east = lane == LANES - 1

    def at(r, c=0):
        return pl.ds((c * cr + r) * SLOTS, SLOTS)

    def west(v):
        return pltpu.roll(v, 1, 0)

    def east(v):
        return pltpu.roll(v, SLOTS - 1, 0)

    def south(v):
        return jnp.where(is_west, 0.0, pltpu.roll(v, 1, 1))

    def north(v):
        return jnp.where(is_east, 0.0, pltpu.roll(v, LANES - 1, 1))

    for r in range(cr):
        lanes = pl.ds((r & 1) * LANES, LANES)
        sums = [acc_s[pl.ds((q * half + r // 2) * SLOTS, SLOTS), lanes] + ext[at(r, q), :] for q in range(3)]
        inverse = 1.0 / (sums[0] + PRIOR_WEIGHT)
        basalt = sums[1] * inverse
        melt = sums[2] * inverse
        comp[0, r] = basalt
        comp[1, r] = melt
        fs[at(r, 2), :] = fs[at(r, 2), :] - BUOYANCY * basalt
        visc[at(r), :] = inside * (bs[at(r), :] * jnp.exp(CONTRAST_BASALT * basalt - CONTRAST_MELT * melt))

    weight_lo = jnp.where(k == 0, 0.5 * RADIAL, RADIAL)
    weight_hi = jnp.where(k == nk - 1, 0.5 * RADIAL, RADIAL)

    def below(r):
        if r == 0:
            return weight_lo * visc[at(0), :]
        return 0.5 * RADIAL * (visc[at(r - 1), :] + visc[at(r), :])

    def above(r):
        if r == cr - 1:
            return weight_hi * visc[at(cr - 1), :]
        return below(r + 1)

    forward = None
    for r in range(cr):
        v = visc[at(r), :]
        scale = LATERAL * 0.5
        fw, fe, fs_, fn = (scale * (v + side(v)) for side in (west, east, south, north))
        f_w[at(r), :] = fw
        f_e[at(r), :] = fe
        f_s[at(r), :] = fs_
        f_n[at(r), :] = fn
        diagonal = fw + fe + fs_ + fn + below(r) + above(r)
        diagonal = jnp.where(v > 0.0, diagonal, 1.0)
        if r > 0:
            diagonal = diagonal - below(r) * up[at(r - 1), :]
        inverse = 1.0 / diagonal
        ip[at(r), :] = inverse
        if r < cr - 1:
            up[at(r), :] = above(r) * inverse
        forward = inverse if r == 0 else below(r) * forward * inverse
        res0[at(r), :] = forward
    backward = ip[at(cr - 1), :]
    backward0 = res0[at(cr - 1), :]
    res1[at(cr - 1), :] = backward
    for r in range(cr - 2, -1, -1):
        u = up[at(r), :]
        backward = u * backward
        res1[at(r), :] = backward
        backward0 = res0[at(r), :] + u * backward0
        res0[at(r), :] = backward0

    def particular(current):
        for c in range(3):
            carried = None
            for r in range(cr):
                v = current[at(r, c), :]
                right = (
                    fs[at(r, c), :]
                    + f_w[at(r), :] * west(v)
                    + f_e[at(r), :] * east(v)
                    + f_s[at(r), :] * south(v)
                    + f_n[at(r), :] * north(v)
                )
                carried = right if r == 0 else right + below(r) * carried
                carried = carried * ip[at(r), :]
                part[at(r, c), :] = carried
            for r in range(cr - 2, -1, -1):
                carried = part[at(r, c), :] + up[at(r), :] * carried
                part[at(r, c), :] = carried

    def exchange(src, dst, size, phase):
        copies = []
        for d in range(1, nk):
            other = lax.rem(k + d, nk)
            n = phase * (nk - 1) + d - 1
            copies.append(
                pltpu.make_async_remote_copy(
                    src_ref=src.at[pl.ds(pl.multiple_of(other * size, 8), size)],
                    dst_ref=dst.at[pl.ds(pl.multiple_of(k * size, 8), size)],
                    send_sem=rad_send.at[n], recv_sem=rad_recv.at[n],
                    device_id=(l, other), device_id_type=MESH,
                )
            )
        for copy in copies:
            copy.start()
        mine = pl.ds(pl.multiple_of(k * size, 8), size)
        dst[mine, :] = src[mine, :]
        return copies

    def to_solvers(dst, size, number, value):
        for t in range(2):
            dst[pl.ds(number * 2 + t, nk, stride=size), :] = value[t * 8:(t + 1) * 8]

    def from_solvers(src, number):
        return jnp.concatenate([src[pl.ds(number * 2 + t, nk, stride=Q2), :] for t in range(2)], 0)

    def piece(src, size, i, number):
        return src[pl.ds(i * size + number * 2, 2), :]

    def apply(answers, store):
        for c in range(3):
            low_flux = from_solvers(answers, c)
            high_flux = from_solvers(answers, 3 + c)
            for r in range(cr):
                value = part[at(r, c), :] + res0[at(r), :] * low_flux + res1[at(r), :] * high_flux
                store(c, r, value)

    def solve(factors, source, size, first, back):
        sums = [piece(source, size, 0, first + 3 + c) for c in range(3)]
        fixed = [[piece(source, size, 0, first + c) for c in range(3)]]
        olds = [None]
        for i in range(1, nk):
            f = factors[i]
            olds.append([s * f["ih"] for s in sums])
            fixed.append([f["cf"] * piece(source, size, i, first + c) + f["cp"] * sums[c] for c in range(3)])
            sums = [
                piece(source, size, i, first + 3 + c) + f["e1"] * sums[c] + f["e2"] * fixed[i][c] for c in range(3)
            ]
        for c in range(3):
            flux = None
            back[pl.ds((nk - 1) * Q2 + (3 + c) * 2, 2), :] = jnp.zeros((2, LANES), F32)
            back[pl.ds(c * 2, 2), :] = jnp.zeros((2, LANES), F32)
            for i in range(nk - 1, 0, -1):
                f = factors[i]
                first_value = fixed[i][c] if flux is None else fixed[i][c] + f["f1"] * flux
                last_value = olds[i][c] + f["qq"] * first_value
                back[pl.ds(i * Q2 + c * 2, 2), :] = f["fb"] * last_value + f["dl"] * first_value
                flux = f["fb"] * first_value - f["dl"] * last_value
                back[pl.ds((i - 1) * Q2 + (3 + c) * 2, 2), :] = flux

    particular(vs)
    for number, value in enumerate(
        [res0[at(0), :], res1[at(0), :], res1[at(cr - 1), :], visc[at(0), :], visc[at(cr - 1), :]]
        + [part[at(0, c), :] for c in range(3)]
        + [part[at(cr - 1, c), :] for c in range(3)]
    ):
        to_solvers(snd1, Q1, number, value)
    sent = exchange(snd1, rcv1, Q1, 0)
    for copy in sent:
        copy.wait_recv()
    everything = early + late + sent

    factors = [None]
    slope = piece(rcv1, Q1, 0, 2)
    for i in range(1, nk):
        a, b, d, v_first = (piece(rcv1, Q1, i, n) for n in (0, 1, 2, 3))
        v_last = piece(rcv1, Q1, i - 1, 4)
        fb = 0.5 * RADIAL * (v_last + v_first)
        dl = 0.5 * RADIAL * (v_first - v_last)
        afb = a * fb
        h = 1.0 + slope * dl
        inverse_h = 1.0 / h
        inverse = 1.0 / (h * (1.0 - a * dl) - afb * (fb * slope))
        qq = fb * slope * inverse_h
        cf = h * inverse
        f1 = cf * b
        e2 = b * (fb * qq + dl)
        factors.append(dict(fb=fb, dl=dl, ih=inverse_h, qq=qq, cf=cf, cp=afb * inverse, f1=f1, e1=b * fb * inverse_h, e2=e2))
        slope = d + e2 * f1
    solve(factors, rcv1, Q1, 5, bck1)
    sent = exchange(bck1, ans1, Q2, 1)
    for copy in sent:
        copy.wait_recv()
    everything += sent

    def store_current(c, r, value):
        vs[at(r, c), :] = value * inside

    apply(ans1, store_current)

    particular(vs)
    for c in range(3):
        to_solvers(snd2, Q2, c, part[at(0, c), :])
        to_solvers(snd2, Q2, 3 + c, part[at(cr - 1, c), :])
    sent = exchange(snd2, rcv2, Q2, 2)
    for copy in sent:
        copy.wait_recv()
    everything += sent
    solve(factors, rcv2, Q2, 0, bck2)
    sent = exchange(bck2, ans2, Q2, 3)
    for copy in sent:
        copy.wait_recv()
    everything += sent

    def store_out(c, r, value):
        out[c, r] = value

    apply(ans2, store_out)
    for copy in everything:
        copy.wait_send()


def solution(mesh):
    nl, nk = mesh.shape["lat"], mesh.shape["rad"]

    def local(tracer_values, tracer_cell, tracer_count, base_viscosity, velocity, forcing):
        cx, cr, ny = base_viscosity.shape
        slots = tracer_cell.shape[2]
        assert nk == 8 and cx + 2 * HALO == SLOTS and ny == LANES and cr == 12
        total_rows = slots // LANES
        vmem = functools.partial(pltpu.VMEM, dtype=F32)
        field = cr * SLOTS
        spare = 8 * SLOTS
        scratch = [
            vmem((3 * total_rows, LANES)), vmem((total_rows, LANES)), vmem((total_rows, LANES)),
            vmem((3 * field // 2, 2 * LANES)),
        ]
        scratch += [vmem((96, LANES))] * 8
        scratch += [vmem((3, HALO, cr, LANES))] * 2 + [vmem((3, 1, cr, LANES))] * 2 + [vmem((HALO, cr, LANES))] * 2
        scratch += [vmem((3 * field + 2 * spare, LANES))] + [vmem((3 * field + spare, LANES))] * 2 + [vmem((field + spare, LANES))]
        scratch += [vmem((field, LANES))] * 9 + [vmem((3 * field, LANES))]
        scratch += [vmem((nk * Q1, LANES))] * 2 + [vmem((nk * Q2, LANES))] * 6
        scratch += [pltpu.SemaphoreType.DMA((10,))] * 2 + [pltpu.SemaphoreType.DMA((4 * (nk - 1),))] * 2
        v = pl.BlockSpec(memory_space=pltpu.VMEM)
        smoothed, composition = pl.pallas_call(
            functools.partial(kernel, nl, nk),
            out_shape=[
                jax.ShapeDtypeStruct((3, cr, SLOTS, ny), F32),
                jax.ShapeDtypeStruct((2, cr, SLOTS, ny), F32),
            ],
            in_specs=[v, v, pl.BlockSpec(memory_space=pltpu.SMEM), v, v, v],
            out_specs=[v, v],
            scratch_shapes=scratch,
            compiler_params=pltpu.CompilerParams(collective_id=0, has_side_effects=True),
        )(
            tracer_values.reshape(3 * total_rows, LANES),
            tracer_cell.reshape(total_rows, LANES),
            tracer_count,
            base_viscosity,
            velocity,
            forcing,
        )
        own = slice(HALO, HALO + cx)
        return (
            jnp.transpose(smoothed[:, :, own], (0, 2, 1, 3)),
            jnp.transpose(composition[:, :, own], (0, 2, 1, 3)),
        )

    return jax.shard_map(
        local,
        mesh=mesh,
        in_specs=(
            P("lat", "rad", None, None),
            P("lat", "rad", None),
            P("lat", "rad", None),
            P("lat", "rad", None),
            P(None, "lat", "rad", None),
            P(None, "lat", "rad", None),
        ),
        out_specs=(P(None, "lat", "rad", None), P(None, "lat", "rad", None)),
        check_vma=False,
    )
```

```python
import functools

import jax
import jax.numpy as jnp
from jax import lax
from jax.experimental import pallas as pl
from jax.experimental.pallas import tpu as pltpu
from jax.sharding import PartitionSpec as P

MESH = pl.DeviceIdType.MESH
F32 = jnp.float32
BF16 = jnp.bfloat16

SWEEPS = 2
LATERAL = 0.015625
RADIAL = 32.0
BUOYANCY = 0.1
PRIOR_WEIGHT = 0.5
CONTRAST_BASALT = 2.3
CONTRAST_MELT = 1.5

SLOTS = 16
HALO = 2
LANES = 128
WINDOW = 8
Q1 = 11 * WINDOW
Q2 = 6 * WINDOW


def side_index(cell, first_plane, cr):
    rows = (cell >> 7) - first_plane * cr
    plane = (rows >= cr).astype(jnp.int32)
    radial = rows - cr * plane
    return (plane * 2 + (radial & 1)) * 8 + (radial >> 1)


def stay_index(cell, cr):
    rows = cell >> 8
    half = cr // 2
    plane = (rows * 43691) >> 18
    return (rows - half * plane) * SLOTS + plane + HALO


def hot_masks(index, tiles):
    base = lax.broadcasted_iota(jnp.int32, (16, LANES), 0).astype(F32)
    return [index == (base + 16.0 * t).astype(BF16) for t in range(tiles)]


def bin_group(acc, loads, index_a, index_b, first_row, rows, step_rows, tiles_a, tiles_b, total_rows):
    zero = jnp.zeros((16, LANES), BF16)
    one = jnp.ones((16, LANES), BF16)

    def spread(ref, row):
        return jnp.broadcast_to(ref[pl.ds(row, 1), :], (16, LANES)).astype(BF16)

    def body(step, carry):
        left, right = [], []
        for j in range(step_rows):
            row = first_row + step * step_rows + j
            values = [spread(loads, q * total_rows + row) for q in range(3)]
            hot_a = hot_masks(spread(index_a, row), tiles_a)
            hot_b = hot_masks(spread(index_b, row), tiles_b)
            left.append(jnp.concatenate([jnp.where(h, v, zero) for v in values for h in hot_a], 0))
            right.append(jnp.concatenate([jnp.where(h, one, zero) for h in hot_b], 0))
        acc[...] += lax.dot_general(
            jnp.concatenate(left, 1),
            jnp.concatenate(right, 1),
            (((1,), (1,)), ((), ())),
            preferred_element_type=F32,
        )
        return carry

    lax.fori_loop(0, rows // step_rows, body, 0)


def kernel(
    nl, nk, vals, cell, cnt, bv, vel, frc, out, comp,
    loads, index_a, index_b, acc_s, acc_side, edge_lo, edge_hi, got_a, got_b, got_c, got_s,
    hv, hf, hb, pv, pf, pb,
    ext, vs, fs, bs, visc, f_w, f_e, f_s, f_n, up, ip, res0, res1, part, mix,
    snd1, rcv1, snd2, rcv2, flux_lo, flux_hi, share, fin, ret,
    lat_send, lat_recv, chip_send, chip_recv, rad_send, rad_recv,
):
    cx, cr = bv.shape[0], bv.shape[1]
    rows_all = 2 * cr
    half = cr // 2
    total_rows = cell.shape[0]
    rows = total_rows // 3
    nc = nk // 2
    l = lax.axis_index("lat")
    k = lax.axis_index("rad")
    kc = k // 2
    par = lax.rem(k, 2)
    lm = lax.rem(l + nl - 1, nl)
    lp = lax.rem(l + 1, nl)
    odd_below = (lm, 2 * kc + 1)
    even_above = (lp, 2 * kc)
    partner = (l, 2 * kc + 1 - par)
    peers = [(l, 2 * lax.rem(kc + d, nc) + par) for d in range(1, nc)]
    window = par * 6

    barrier = pltpu.get_barrier_semaphore()
    beside = lm + par * (lp - lm)
    for device in [(beside, 2 * kc), (beside, 2 * kc + 1), partner] + peers:
        pl.semaphore_signal(barrier, inc=1, device_id=device, device_id_type=MESH)

    def remote(src, dst, device, send, recv):
        return pltpu.make_async_remote_copy(
            src_ref=src, dst_ref=dst, send_sem=send, recv_sem=recv, device_id=device, device_id_type=MESH
        )

    def to_lat(low, high, dst, n):
        return [
            remote(low, dst.at[par], odd_below, lat_send.at[n], lat_recv.at[2 * (n // 2) + par]),
            remote(high, dst.at[par], even_above, lat_send.at[n + 1], lat_recv.at[2 * (n // 2) + par]),
        ]

    def from_lat(dst, n):
        for p in range(2):
            remote(dst.at[p], dst.at[p], partner, lat_send.at[n + p], lat_recv.at[n + p]).wait_recv()

    def to_partner(src, dst, n):
        return remote(src, dst, partner, chip_send.at[n], chip_recv.at[n])

    place = lax.broadcasted_iota(jnp.int32, (rows, LANES), 0) * LANES + lax.broadcasted_iota(
        jnp.int32, (rows, LANES), 1
    )
    for g in (0, 2, 1):
        sl = pl.ds(g * rows, rows)
        weight = jnp.where(place < cnt[0, 0, g], 0.5 + vals[sl, :], 0.0)
        loads[sl, :] = weight
        loads[pl.ds(total_rows + g * rows, rows), :] = weight * vals[pl.ds(total_rows + g * rows, rows), :]
        loads[pl.ds(2 * total_rows + g * rows, rows), :] = weight * vals[pl.ds(2 * total_rows + g * rows, rows), :]
        c = cell[sl, :]
        if g == 1:
            index_a[sl, :] = stay_index(c, cr).astype(F32)
            index_b[sl, :] = (c & 255).astype(F32)
        else:
            index_a[sl, :] = side_index(c, cx - HALO if g == 0 else 0, cr).astype(F32)
            index_b[sl, :] = (c & 127).astype(F32)

    pl.semaphore_wait(barrier, 3 + len(peers))
    copies = [to_partner(vel, pv, 0), to_partner(frc, pf, 1), to_partner(bv, pb, 2)]
    copies += to_lat(vel.at[:, pl.ds(0, HALO)], vel.at[:, pl.ds(cx - HALO, HALO)], hv, 0)
    copies += to_lat(frc.at[:, pl.ds(0, 1)], frc.at[:, pl.ds(cx - 1, 1)], hf, 2)
    copies += to_lat(bv.at[pl.ds(0, HALO)], bv.at[pl.ds(cx - HALO, HALO)], hb, 4)
    for copy in copies:
        copy.start()

    step_rows = min(32, rows)
    acc_side[...] = jnp.zeros_like(acc_side)
    acc_s[...] = jnp.zeros_like(acc_s)
    bin_group(acc_side.at[0], loads, index_a, index_b, 0, rows, step_rows, 2, 8, total_rows)
    bin_group(acc_side.at[1], loads, index_a, index_b, 2 * rows, rows, step_rows, 2, 8, total_rows)
    sides = to_lat(acc_side.at[0], acc_side.at[1], got_a, 6) + [to_partner(acc_side.at[1 - par], got_c, 3)]
    for copy in sides:
        copy.start()
    bin_group(acc_s, loads, index_a, index_b, rows, rows, step_rows, 6, 16, total_rows)

    for q in range(3):
        for h in range(2):
            for s in range(HALO):
                row = q * 32 + (s * 2 + h) * 8
                lanes = pl.ds(h * LANES, LANES)
                edge_lo[pl.ds(row, 8), :] = jnp.zeros((8, LANES), F32)
                edge_hi[pl.ds(row, 8), :] = jnp.zeros((8, LANES), F32)
                for p in range(half):
                    base = q * half * SLOTS + p * SLOTS
                    edge_lo[pl.ds(row + p, 1), :] = acc_s[pl.ds(base + HALO + s, 1), lanes]
                    edge_hi[pl.ds(row + p, 1), :] = acc_s[pl.ds(base + HALO + cx - HALO + s, 1), lanes]
    late = to_lat(edge_lo, edge_hi, got_b, 8) + [to_partner(acc_s, got_s, 4)]
    for copy in late:
        copy.start()
    copies += sides + late

    field = rows_all * SLOTS

    def put(dst, c, parity, slot, value):
        dst[pl.ds(c * field + parity * cr * SLOTS + slot, cr, stride=SLOTS), :] = value

    near = par * (SLOTS - HALO)
    keep = jnp.where(l + par * (nl - 1) == par * 2 * (nl - 1), 0.0, 1.0)
    ext[...] = jnp.zeros_like(ext)
    for n in range(3):
        copies[n].wait_recv()
    for x in range(cx):
        put(bs, 0, par, x + HALO, bv[x])
        put(bs, 0, 1 - par, x + HALO, pb[x])
        for c in range(3):
            put(vs, c, par, x + HALO, vel[c, x])
            put(vs, c, 1 - par, x + HALO, pv[c, x])
            put(fs, c, par, x + HALO, frc[c, x])
            put(fs, c, 1 - par, x + HALO, pf[c, x])
    from_lat(hv, 0)
    from_lat(hf, 2)
    from_lat(hb, 4)
    for p in range(2):
        for s in range(HALO):
            put(bs, 0, p, near + s, hb[p, s])
            for c in range(3):
                put(vs, c, p, near + s, hv[p, c, s] * keep)
        for c in range(3):
            put(fs, c, p, 1 + par * (SLOTS - 3), hf[p, c, 0])

    def put_edge(ref, parity, slot, scale):
        for q in range(3):
            for h in range(2):
                for s in range(HALO):
                    value = ref[pl.ds(q * 32 + (s * 2 + h) * 8, half), :] * scale
                    start = q * field + (parity * cr + h) * SLOTS + slot + s
                    ext[pl.ds(start, half, stride=2 * SLOTS), :] = value

    from_lat(got_a, 6)
    for p in range(2):
        put_edge(got_a.at[p], p, HALO + par * (SLOTS - 3 * HALO), keep)
    sides[2].wait_recv()
    from_lat(got_b, 8)
    got_b[par] = got_b[par] + acc_side[par]
    got_b[1 - par] = got_b[1 - par] + got_c[...]
    for p in range(2):
        put_edge(got_b.at[p], p, near, 1.0)
    late[2].wait_recv()

    slot_of = lax.broadcasted_iota(jnp.int32, (SLOTS, LANES), 0)
    lane = lax.broadcasted_iota(jnp.int32, (WINDOW, LANES), 1)
    low = jnp.where(l == 0, HALO, 0)
    high = jnp.where(l == nl - 1, SLOTS - HALO, SLOTS)
    inside = jnp.where((slot_of >= low) & (slot_of < high), 1.0, 0.0)
    slot_here = lax.broadcasted_iota(jnp.int32, (WINDOW, LANES), 0) + window + 1
    inside_here = jnp.where((slot_here >= low) & (slot_here < high), 1.0, 0.0)
    is_south = lane == 0
    is_north = lane == LANES - 1

    def by_slot(R, c=0):
        return pl.ds((c * rows_all + R) * SLOTS, SLOTS)

    def near_slot(R, shift, c=0):
        return pl.ds((c * rows_all + R) * SLOTS + window + shift, WINDOW)

    def at(R, c=0):
        return pl.ds((c * rows_all + R) * WINDOW, WINDOW)

    def south(v):
        return jnp.where(is_south, 0.0, pltpu.roll(v, 1, 1))

    def north(v):
        return jnp.where(is_north, 0.0, pltpu.roll(v, LANES - 1, 1))

    for whose, ref in ((par, acc_s), (1 - par, got_s)):
        for r in range(cr):
            lanes = pl.ds((r & 1) * LANES, LANES)
            sums = []
            for q in range(3):
                more = ext[pl.ds(pl.multiple_of(q * field + (whose * cr + r) * SLOTS, 8), SLOTS), :]
                sums.append(ref[pl.ds((q * half + r // 2) * SLOTS, SLOTS), lanes] + more)
            inverse = 1.0 / (sums[0] + PRIOR_WEIGHT)
            basalt = sums[1] * inverse
            melt = sums[2] * inverse
            here = pl.ds(pl.multiple_of((whose * cr + r) * SLOTS, 8), SLOTS)
            mix[here, :] = basalt
            mix[pl.ds(pl.multiple_of(field + (whose * cr + r) * SLOTS, 8), SLOTS), :] = melt
            heavy = pl.ds(pl.multiple_of(2 * field + (whose * cr + r) * SLOTS, 8), SLOTS)
            fs[heavy, :] = fs[heavy, :] - BUOYANCY * basalt
            visc[here, :] = inside * (bs[here, :] * jnp.exp(CONTRAST_BASALT * basalt - CONTRAST_MELT * melt))

    weight_lo = jnp.where(kc == 0, 0.5 * RADIAL, RADIAL)
    weight_hi = jnp.where(kc == nc - 1, 0.5 * RADIAL, RADIAL)
    top = rows_all - 1
    v_at = [visc[near_slot(R, 1), :] for R in range(rows_all)]
    face = [weight_lo * v_at[0]]
    face += [0.5 * RADIAL * (v_at[R - 1] + v_at[R]) for R in range(1, rows_all)]
    face += [weight_hi * v_at[top]]
    face_ref = share
    for R in range(rows_all + 1):
        face_ref[pl.ds(R * WINDOW, WINDOW), :] = face[R]

    def below(R):
        return face_ref[pl.ds(R * WINDOW, WINDOW), :]

    def above(R):
        return below(R + 1)

    def diagonal(R):
        v = visc[near_slot(R, 1), :]
        scale = LATERAL * 0.5
        fw = scale * (v + visc[near_slot(R, 0), :])
        fe = scale * (v + visc[near_slot(R, 2), :])
        fs_, fn = scale * (v + south(v)), scale * (v + north(v))
        f_w[at(R), :] = fw
        f_e[at(R), :] = fe
        f_s[at(R), :] = fs_
        f_n[at(R), :] = fn
        return jnp.where(v > 0.0, fw + fe + fs_ + fn + below(R) + above(R), 1.0)

    u_low = u_high = m_low = m_high = None
    for n in range(cr):
        lo, hi = n, top - n
        p_low, p_high = diagonal(lo), diagonal(hi)
        if n > 0:
            p_low = p_low - below(lo) * u_low
            p_high = p_high - above(hi) * u_high
        i_low, i_high = 1.0 / p_low, 1.0 / p_high
        ip[at(lo), :] = i_low
        ip[at(hi), :] = i_high
        m_low = i_low if n == 0 else below(lo) * m_low * i_low
        m_high = i_high if n == 0 else above(hi) * m_high * i_high
        res0[at(lo), :] = m_low
        res1[at(hi), :] = m_high
        u_low, u_high = above(lo) * i_low, below(hi) * i_high
        up[at(lo), :] = u_low
        up[at(hi), :] = u_high
    middle = 1.0 / (1.0 - u_low * u_high)

    x0, y1 = m_low * middle, m_high * middle
    y0, x1 = u_high * x0, u_low * y1
    for n in range(cr - 1, -1, -1):
        lo, hi = n, top - n
        if n < cr - 1:
            x0 = res0[at(lo), :] + up[at(lo), :] * x0
            x1 = up[at(lo), :] * x1
            y0 = up[at(hi), :] * y0
            y1 = res1[at(hi), :] + up[at(hi), :] * y1
        res0[at(lo), :] = x0
        res1[at(lo), :] = x1
        res0[at(hi), :] = y0
        res1[at(hi), :] = y1

    def right_side(R, c):
        v = vs[near_slot(R, 1, c), :]
        return (
            fs[near_slot(R, 1, c), :]
            + f_w[at(R), :] * vs[near_slot(R, 0, c), :]
            + f_e[at(R), :] * vs[near_slot(R, 2, c), :]
            + f_s[at(R), :] * south(v)
            + f_n[at(R), :] * north(v)
        )

    def particular():
        low_m, high_m = [None] * 3, [None] * 3
        for n in range(cr):
            lo, hi = n, top - n
            for c in range(3):
                a, b = right_side(lo, c), right_side(hi, c)
                if n > 0:
                    a = a + below(lo) * low_m[c]
                    b = b + above(hi) * high_m[c]
                low_m[c] = a * ip[at(lo), :]
                high_m[c] = b * ip[at(hi), :]
                part[at(lo, c), :] = low_m[c]
                part[at(hi, c), :] = high_m[c]
        for c in range(3):
            x = (low_m[c] + u_low * high_m[c]) * middle
            y = high_m[c] + u_high * x
            part[at(cr - 1, c), :] = x
            part[at(cr, c), :] = y
            for n in range(cr - 2, -1, -1):
                lo, hi = n, top - n
                x = part[at(lo, c), :] + up[at(lo), :] * x
                y = part[at(hi, c), :] + up[at(hi), :] * y
                part[at(lo, c), :] = x
                part[at(hi, c), :] = y

    def gather(src, dst, phase):
        sent = []
        for d in (2, 1, 3):
            n = phase * (nc - 1) + d - 1
            sent.append(remote(src, dst.at[kc], peers[d - 1], rad_send.at[n], rad_recv.at[n]))
        for copy in sent:
            copy.start()
        dst[kc] = src[...]
        return sent

    def piece(source, i, number):
        return source[i, pl.ds(number * WINDOW, WINDOW), :]

    def solve(factors, source, first):
        sums = [piece(source, 0, first + 3 + c) for c in range(3)]
        fixed = [[piece(source, 0, first + c) for c in range(3)]]
        olds = [None]
        for i in range(1, nc):
            f = factors[i]
            olds.append([s * f["ih"] for s in sums])
            fixed.append([f["cf"] * piece(source, i, first + c) + f["cp"] * sums[c] for c in range(3)])
            sums = [piece(source, i, first + 3 + c) + f["e1"] * sums[c] + f["e2"] * fixed[i][c] for c in range(3)]
        for c in range(3):
            flux = None
            flux_hi[nc - 1, c] = jnp.zeros((WINDOW, LANES), F32)
            flux_lo[0, c] = jnp.zeros((WINDOW, LANES), F32)
            for i in range(nc - 1, 0, -1):
                f = factors[i]
                first_value = fixed[i][c] if flux is None else fixed[i][c] + f["f1"] * flux
                last_value = olds[i][c] + f["qq"] * first_value
                flux_lo[i, c] = f["fb"] * last_value + f["dl"] * first_value
                flux = f["fb"] * first_value - f["dl"] * last_value
                flux_hi[i - 1, c] = flux

    def solved(R, c):
        return part[at(R, c), :] + res0[at(R), :] * flux_lo[kc, c] + res1[at(R), :] * flux_hi[kc, c]

    particular()
    for number, value in enumerate(
        [res0[at(0), :], res1[at(0), :], res1[at(top), :], v_at[0], v_at[top]]
        + [part[at(0, c), :] for c in range(3)]
        + [part[at(top, c), :] for c in range(3)]
    ):
        snd1[pl.ds(number * WINDOW, WINDOW), :] = value
    sent = gather(snd1, rcv1, 0)
    copies += sent

    for c in range(2):
        for R in range(rows_all):
            fin[pl.ds((c * rows_all + R) * WINDOW, WINDOW), :] = mix[near_slot(R, 1, c), :]

    def give(n, fields, first):
        made = []
        for c in range(fields):
            theirs = pl.ds(pl.multiple_of(((first + c) * rows_all + (1 - par) * cr) * WINDOW, 8), cr * WINDOW)
            made.append(to_partner(fin.at[theirs], ret.at[first + c, pl.ds(0, cr * WINDOW)], n + c))
        for copy in made:
            copy.start()
        return made

    shared = give(5, 2, 0)
    for copy in shared:
        copy.wait_recv()
    copies += shared

    def collect(field, store):
        for i in range(1, 1 + cx // 2):
            mine = fin[pl.ds((field * rows_all + par * cr) * WINDOW + i, cr, stride=WINDOW), :]
            theirs = ret[field, pl.ds(i, cr, stride=WINDOW), :]
            store(par * (cx // 2) + i - 1, mine)
            store((1 - par) * (cx // 2) + i - 1, theirs)

    for c in range(2):
        collect(c, lambda x, value: comp.__setitem__((pl.ds(x * 2 * cr + c, cr, stride=2), slice(None)), value))
    for copy in sent:
        copy.wait_recv()

    factors = [None]
    slope = piece(rcv1, 0, 2)
    for i in range(1, nc):
        a, b, d, v_first = (piece(rcv1, i, n) for n in (0, 1, 2, 3))
        v_last = piece(rcv1, i - 1, 4)
        fb = 0.5 * RADIAL * (v_last + v_first)
        dl = 0.5 * RADIAL * (v_first - v_last)
        afb = a * fb
        h = 1.0 + slope * dl
        inverse_h = 1.0 / h
        inverse = 1.0 / (h * (1.0 - a * dl) - afb * (fb * slope))
        qq = fb * slope * inverse_h
        cf = h * inverse
        f1 = cf * b
        e2 = b * (fb * qq + dl)
        factors.append(dict(fb=fb, dl=dl, ih=inverse_h, qq=qq, cf=cf, cp=afb * inverse, f1=f1, e1=b * fb * inverse_h, e2=e2))
        slope = d + e2 * f1
    solve(factors, rcv1, 5)
    for c in range(3):
        for R in range(rows_all):
            vs[near_slot(R, 1, c), :] = solved(R, c) * inside_here

    particular()
    for c in range(3):
        snd2[pl.ds(c * WINDOW, WINDOW), :] = part[at(0, c), :]
        snd2[pl.ds((3 + c) * WINDOW, WINDOW), :] = part[at(top, c), :]
    sent = gather(snd2, rcv2, 1)
    for copy in sent:
        copy.wait_recv()
    copies += sent
    solve(factors, rcv2, 0)
    for c in range(3):
        for R in range(rows_all):
            fin[pl.ds(((2 + c) * rows_all + R) * WINDOW, WINDOW), :] = solved(R, c)
    shared = give(7, 3, 2)
    for copy in shared:
        copy.wait_recv()
    copies += shared
    for c in range(3):
        collect(2 + c, lambda x, value: out.__setitem__((c, x), value))
    for copy in copies:
        copy.wait_send()


def solution(mesh):
    nl, nk = mesh.shape["lat"], mesh.shape["rad"]

    def local(tracer_values, tracer_cell, tracer_count, base_viscosity, velocity, forcing):
        cx, cr, ny = base_viscosity.shape
        slots = tracer_cell.shape[2]
        assert nk == 8 and cx + 2 * HALO == SLOTS and ny == LANES and cr == 12
        total_rows = slots // LANES
        vmem = functools.partial(pltpu.VMEM, dtype=F32)
        field = 2 * cr * SLOTS
        compact = 2 * cr * WINDOW
        spare = 8 * SLOTS
        nc = nk // 2
        scratch = [
            vmem((3 * total_rows, LANES)), vmem((total_rows, LANES)), vmem((total_rows, LANES)),
            vmem((3 * (cr // 2) * SLOTS, 2 * LANES)), vmem((2, 96, LANES)), vmem((96, LANES)), vmem((96, LANES)),
            vmem((2, 96, LANES)), vmem((2, 96, LANES)), vmem((96, LANES)), vmem((3 * (cr // 2) * SLOTS, 2 * LANES)),
            vmem((2, 3, HALO, cr, LANES)), vmem((2, 3, 1, cr, LANES)), vmem((2, HALO, cr, LANES)),
            vmem((3, cx, cr, LANES)), vmem((3, cx, cr, LANES)), vmem((cx, cr, LANES)),
            vmem((3 * field + 2 * spare, LANES)), vmem((3 * field + spare, LANES)), vmem((3 * field + spare, LANES)),
            vmem((field + spare, LANES)), vmem((field, LANES)),
        ]
        scratch += [vmem((compact, LANES))] * 8 + [vmem((3 * compact, LANES)), vmem((2 * field, LANES))]
        scratch += [vmem((Q1, LANES)), vmem((nc, Q1, LANES)), vmem((Q2, LANES)), vmem((nc, Q2, LANES))]
        scratch += [vmem((nc, 3, WINDOW, LANES))] * 2 + [vmem((compact + WINDOW, LANES))]
        scratch += [vmem((5 * compact + spare, LANES)), vmem((5, cr * WINDOW + 8 * WINDOW, LANES))]
        scratch += [pltpu.SemaphoreType.DMA((n,)) for n in (10, 10, 10, 10, 2 * (nc - 1), 2 * (nc - 1))]
        v = pl.BlockSpec(memory_space=pltpu.VMEM)
        smoothed, composition = pl.pallas_call(
            functools.partial(kernel, nl, nk),
            out_shape=[
                jax.ShapeDtypeStruct((3, cx, cr, ny), F32),
                jax.ShapeDtypeStruct((cx * cr * 2, ny), F32),
            ],
            in_specs=[v, v, pl.BlockSpec(memory_space=pltpu.SMEM), v, v, v],
            out_specs=[v, v],
            scratch_shapes=scratch,
            compiler_params=pltpu.CompilerParams(collective_id=0, has_side_effects=True),
        )(
            tracer_values.reshape(3 * total_rows, LANES),
            tracer_cell.reshape(total_rows, LANES),
            tracer_count,
            base_viscosity,
            velocity,
            forcing,
        )
        return smoothed, jnp.transpose(composition.reshape(cx, cr, 2, ny), (2, 0, 1, 3))

    return jax.shard_map(
        local,
        mesh=mesh,
        in_specs=(
            P("lat", "rad", None, None),
            P("lat", "rad", None),
            P("lat", "rad", None),
            P("lat", "rad", None),
            P(None, "lat", "rad", None),
            P(None, "lat", "rad", None),
        ),
        out_specs=(P(None, "lat", "rad", None), P(None, "lat", "rad", None)),
        check_vma=False,
    )
```

```python
import functools

import jax
import jax.numpy as jnp
from jax import lax
from jax.experimental import pallas as pl
from jax.experimental.pallas import tpu as pltpu
from jax.sharding import PartitionSpec as P

MESH = pl.DeviceIdType.MESH
F32 = jnp.float32
BF16 = jnp.bfloat16

SWEEPS = 2
LATERAL = 0.015625
RADIAL = 32.0
BUOYANCY = 0.1
PRIOR_WEIGHT = 0.5
CONTRAST_BASALT = 2.3
CONTRAST_MELT = 1.5

SLOTS = 16
HALO = 2
LANES = 128
WINDOW = 8
Q1 = 11 * WINDOW
Q2 = 6 * WINDOW


def side_index(cell, first_plane, cr):
    rows = (cell >> 7) - first_plane * cr
    plane = (rows >= cr).astype(jnp.int32)
    radial = rows - cr * plane
    return (plane * 2 + (radial & 1)) * 8 + (radial >> 1)


def stay_index(cell, cr):
    rows = cell >> 8
    half = cr // 2
    plane = (rows * 43691) >> 18
    return (rows - half * plane) * SLOTS + plane + HALO


def hot_masks(index, tiles):
    base = lax.broadcasted_iota(jnp.int32, (16, LANES), 0).astype(F32)
    return [index == (base + 16.0 * t).astype(BF16) for t in range(tiles)]


def bin_group(acc, loads, index_a, index_b, first_row, rows, step_rows, tiles_a, tiles_b, total_rows):
    zero = jnp.zeros((16, LANES), BF16)
    one = jnp.ones((16, LANES), BF16)

    def spread(ref, row):
        return jnp.broadcast_to(ref[pl.ds(row, 1), :], (16, LANES)).astype(BF16)

    def body(step, carry):
        left, right = [], []
        for j in range(step_rows):
            row = first_row + step * step_rows + j
            values = [spread(loads, q * total_rows + row) for q in range(3)]
            hot_a = hot_masks(spread(index_a, row), tiles_a)
            hot_b = hot_masks(spread(index_b, row), tiles_b)
            left.append(jnp.concatenate([jnp.where(h, v, zero) for v in values for h in hot_a], 0))
            right.append(jnp.concatenate([jnp.where(h, one, zero) for h in hot_b], 0))
        acc[...] += lax.dot_general(
            jnp.concatenate(left, 1),
            jnp.concatenate(right, 1),
            (((1,), (1,)), ((), ())),
            preferred_element_type=F32,
        )
        return carry

    lax.fori_loop(0, rows // step_rows, body, 0)


def kernel(
    nl, nk, vals, cell, cnt, bv, vel, frc, out, comp,
    loads, index_a, index_b, acc_s, acc_side, edge_lo, edge_hi, got_a, got_b, got_c, got_s,
    hv, hf, hb, pv, pf, pb,
    ext, vs, fs, bs, visc, f_w, f_e, f_s, f_n, up, ip, res0, res1, part, mix,
    snd1, rcv1, snd2, rcv2, flux_lo, flux_hi, share, fin, ret,
    lat_send, lat_recv, chip_send, chip_recv, rad_send, rad_recv,
):
    cx, cr = bv.shape[0], bv.shape[1]
    rows_all = 2 * cr
    half = cr // 2
    total_rows = cell.shape[0]
    rows = total_rows // 3
    nc = nk // 2
    l = lax.axis_index("lat")
    k = lax.axis_index("rad")
    kc = k // 2
    par = lax.rem(k, 2)
    lm = lax.rem(l + nl - 1, nl)
    lp = lax.rem(l + 1, nl)
    odd_below = (lm, 2 * kc + 1)
    even_above = (lp, 2 * kc)
    partner = (l, 2 * kc + 1 - par)
    peers = [(l, 2 * lax.rem(kc + d, nc) + par) for d in range(1, nc)]
    window = par * 6

    has_below = l > 0
    has_above = l < nl - 1
    has_beside = l != par * (nl - 1)

    barrier = pltpu.get_barrier_semaphore()
    beside = lm + par * (lp - lm)
    for device in [partner] + peers:
        pl.semaphore_signal(barrier, inc=1, device_id=device, device_id_type=MESH)

    @pl.when(has_beside)
    def _():
        for p in range(2):
            pl.semaphore_signal(barrier, inc=1, device_id=(beside, 2 * kc + p), device_id_type=MESH)

    def remote(src, dst, device, send, recv):
        return pltpu.make_async_remote_copy(
            src_ref=src, dst_ref=dst, send_sem=send, recv_sem=recv, device_id=device, device_id_type=MESH
        )

    def to_lat(low, high, dst, n):
        return [
            (has_below, remote(low, dst.at[par], odd_below, lat_send.at[n], lat_recv.at[n + par])),
            (has_above, remote(high, dst.at[par], even_above, lat_send.at[n + 1], lat_recv.at[n + par])),
        ]

    def start(entries):
        for condition, copy in entries:
            if condition is None:
                copy.start()
            else:
                pl.when(condition)(copy.start)

    def from_lat(pairs):
        @pl.when(has_beside)
        def _():
            for dst, n in pairs:
                for p in range(2):
                    remote(dst.at[p], dst.at[p], partner, lat_send.at[n + p], lat_recv.at[n + p]).wait_recv()

    def to_partner(src, dst, n):
        return (None, remote(src, dst, partner, chip_send.at[n], chip_recv.at[n]))

    place = lax.broadcasted_iota(jnp.int32, (rows, LANES), 0) * LANES + lax.broadcasted_iota(
        jnp.int32, (rows, LANES), 1
    )
    for g in (0, 2, 1):
        sl = pl.ds(g * rows, rows)
        weight = jnp.where(place < cnt[0, 0, g], 0.5 + vals[sl, :], 0.0)
        loads[sl, :] = weight
        loads[pl.ds(total_rows + g * rows, rows), :] = weight * vals[pl.ds(total_rows + g * rows, rows), :]
        loads[pl.ds(2 * total_rows + g * rows, rows), :] = weight * vals[pl.ds(2 * total_rows + g * rows, rows), :]
        c = cell[sl, :]
        if g == 1:
            index_a[sl, :] = stay_index(c, cr).astype(F32)
            index_b[sl, :] = (c & 255).astype(F32)
        else:
            index_a[sl, :] = side_index(c, cx - HALO if g == 0 else 0, cr).astype(F32)
            index_b[sl, :] = (c & 127).astype(F32)

    pl.semaphore_wait(barrier, 1 + len(peers) + jnp.where(has_below, 1, 0) + jnp.where(has_above, 1, 0))
    copies = [to_partner(vel, pv, 0), to_partner(frc, pf, 1), to_partner(bv, pb, 2)]
    copies += to_lat(vel.at[:, pl.ds(0, HALO)], vel.at[:, pl.ds(cx - HALO, HALO)], hv, 0)
    copies += to_lat(frc.at[:, pl.ds(0, 1)], frc.at[:, pl.ds(cx - 1, 1)], hf, 2)
    copies += to_lat(bv.at[pl.ds(0, HALO)], bv.at[pl.ds(cx - HALO, HALO)], hb, 4)
    start(copies)

    step_rows = min(32, rows)
    acc_side[...] = jnp.zeros_like(acc_side)
    acc_s[...] = jnp.zeros_like(acc_s)
    bin_group(acc_side.at[0], loads, index_a, index_b, 0, rows, step_rows, 2, 8, total_rows)
    bin_group(acc_side.at[1], loads, index_a, index_b, 2 * rows, rows, step_rows, 2, 8, total_rows)
    sides = to_lat(acc_side.at[0], acc_side.at[1], got_a, 6) + [to_partner(acc_side.at[1 - par], got_c, 3)]
    start(sides)
    bin_group(acc_s, loads, index_a, index_b, rows, rows, step_rows, 6, 16, total_rows)

    for q in range(3):
        for h in range(2):
            for s in range(HALO):
                row = q * 32 + (s * 2 + h) * 8
                lanes = pl.ds(h * LANES, LANES)
                edge_lo[pl.ds(row, 8), :] = jnp.zeros((8, LANES), F32)
                edge_hi[pl.ds(row, 8), :] = jnp.zeros((8, LANES), F32)
                for p in range(half):
                    base = q * half * SLOTS + p * SLOTS
                    edge_lo[pl.ds(row + p, 1), :] = acc_s[pl.ds(base + HALO + s, 1), lanes]
                    edge_hi[pl.ds(row + p, 1), :] = acc_s[pl.ds(base + HALO + cx - HALO + s, 1), lanes]
    late = to_lat(edge_lo, edge_hi, got_b, 8) + [to_partner(acc_s, got_s, 4)]
    start(late)
    copies += sides + late

    field = rows_all * SLOTS

    def put(dst, c, parity, slot, value):
        dst[pl.ds(c * field + parity * cr * SLOTS + slot, cr, stride=SLOTS), :] = value

    near = par * (SLOTS - HALO)

    def kept(value):
        return jnp.where(has_beside, value, 0.0)

    ext[...] = jnp.zeros_like(ext)
    for n in range(3):
        copies[n][1].wait_recv()
    for x in range(cx):
        put(bs, 0, par, x + HALO, bv[x])
        put(bs, 0, 1 - par, x + HALO, pb[x])
        for c in range(3):
            put(vs, c, par, x + HALO, vel[c, x])
            put(vs, c, 1 - par, x + HALO, pv[c, x])
            put(fs, c, par, x + HALO, frc[c, x])
            put(fs, c, 1 - par, x + HALO, pf[c, x])
    from_lat([(hv, 0), (hf, 2), (hb, 4)])
    for p in range(2):
        for s in range(HALO):
            put(bs, 0, p, near + s, kept(hb[p, s]))
            for c in range(3):
                put(vs, c, p, near + s, kept(hv[p, c, s]))
        for c in range(3):
            put(fs, c, p, 1 + par * (SLOTS - 3), kept(hf[p, c, 0]))

    def put_edge(ref, parity, slot):
        for q in range(3):
            for h in range(2):
                for s in range(HALO):
                    value = ref[pl.ds(q * 32 + (s * 2 + h) * 8, half), :]
                    start = q * field + (parity * cr + h) * SLOTS + slot + s
                    ext[pl.ds(start, half, stride=2 * SLOTS), :] = value

    from_lat([(got_a, 6)])
    for p in range(2):
        got_a[p] = kept(got_a[p])
        put_edge(got_a.at[p], p, HALO + par * (SLOTS - 3 * HALO))
    sides[2][1].wait_recv()
    from_lat([(got_b, 8)])
    got_b[par] = kept(got_b[par]) + acc_side[par]
    got_b[1 - par] = kept(got_b[1 - par]) + got_c[...]
    for p in range(2):
        put_edge(got_b.at[p], p, near)
    late[2][1].wait_recv()

    slot_of = lax.broadcasted_iota(jnp.int32, (SLOTS, LANES), 0)
    lane = lax.broadcasted_iota(jnp.int32, (WINDOW, LANES), 1)
    low = jnp.where(l == 0, HALO, 0)
    high = jnp.where(l == nl - 1, SLOTS - HALO, SLOTS)
    inside = (slot_of >= low) & (slot_of < high)
    slot_here = lax.broadcasted_iota(jnp.int32, (WINDOW, LANES), 0) + window + 1
    inside_here = (slot_here >= low) & (slot_here < high)
    is_south = lane == 0
    is_north = lane == LANES - 1

    def by_slot(R, c=0):
        return pl.ds((c * rows_all + R) * SLOTS, SLOTS)

    def near_slot(R, shift, c=0):
        return pl.ds((c * rows_all + R) * SLOTS + window + shift, WINDOW)

    def at(R, c=0):
        return pl.ds((c * rows_all + R) * WINDOW, WINDOW)

    def south(v):
        return jnp.where(is_south, 0.0, pltpu.roll(v, 1, 1))

    def north(v):
        return jnp.where(is_north, 0.0, pltpu.roll(v, LANES - 1, 1))

    for whose, ref in ((par, acc_s), (1 - par, got_s)):
        for r in range(cr):
            lanes = pl.ds((r & 1) * LANES, LANES)
            sums = []
            for q in range(3):
                more = ext[pl.ds(pl.multiple_of(q * field + (whose * cr + r) * SLOTS, 8), SLOTS), :]
                sums.append(ref[pl.ds((q * half + r // 2) * SLOTS, SLOTS), lanes] + more)
            inverse = 1.0 / (sums[0] + PRIOR_WEIGHT)
            basalt = sums[1] * inverse
            melt = sums[2] * inverse
            here = pl.ds(pl.multiple_of((whose * cr + r) * SLOTS, 8), SLOTS)
            mix[here, :] = basalt
            mix[pl.ds(pl.multiple_of(field + (whose * cr + r) * SLOTS, 8), SLOTS), :] = melt
            heavy = pl.ds(pl.multiple_of(2 * field + (whose * cr + r) * SLOTS, 8), SLOTS)
            fs[heavy, :] = fs[heavy, :] - BUOYANCY * basalt
            visc[here, :] = jnp.where(
                inside, bs[here, :] * jnp.exp(CONTRAST_BASALT * basalt - CONTRAST_MELT * melt), 0.0
            )

    weight_lo = jnp.where(kc == 0, 0.5 * RADIAL, RADIAL)
    weight_hi = jnp.where(kc == nc - 1, 0.5 * RADIAL, RADIAL)
    top = rows_all - 1
    v_at = [visc[near_slot(R, 1), :] for R in range(rows_all)]
    face = [weight_lo * v_at[0]]
    face += [0.5 * RADIAL * (v_at[R - 1] + v_at[R]) for R in range(1, rows_all)]
    face += [weight_hi * v_at[top]]
    face_ref = share
    for R in range(rows_all + 1):
        face_ref[pl.ds(R * WINDOW, WINDOW), :] = face[R]

    def below(R):
        return face_ref[pl.ds(R * WINDOW, WINDOW), :]

    def above(R):
        return below(R + 1)

    def diagonal(R):
        v = visc[near_slot(R, 1), :]
        scale = LATERAL * 0.5
        fw = scale * (v + visc[near_slot(R, 0), :])
        fe = scale * (v + visc[near_slot(R, 2), :])
        fs_, fn = scale * (v + south(v)), scale * (v + north(v))
        f_w[at(R), :] = fw
        f_e[at(R), :] = fe
        f_s[at(R), :] = fs_
        f_n[at(R), :] = fn
        return jnp.where(v > 0.0, fw + fe + fs_ + fn + below(R) + above(R), 1.0)

    u_low = u_high = m_low = m_high = None
    for n in range(cr):
        lo, hi = n, top - n
        p_low, p_high = diagonal(lo), diagonal(hi)
        if n > 0:
            p_low = p_low - below(lo) * u_low
            p_high = p_high - above(hi) * u_high
        i_low, i_high = 1.0 / p_low, 1.0 / p_high
        ip[at(lo), :] = i_low
        ip[at(hi), :] = i_high
        m_low = i_low if n == 0 else below(lo) * m_low * i_low
        m_high = i_high if n == 0 else above(hi) * m_high * i_high
        res0[at(lo), :] = m_low
        res1[at(hi), :] = m_high
        u_low, u_high = above(lo) * i_low, below(hi) * i_high
        up[at(lo), :] = u_low
        up[at(hi), :] = u_high
    middle = 1.0 / (1.0 - u_low * u_high)

    x0, y1 = m_low * middle, m_high * middle
    y0, x1 = u_high * x0, u_low * y1
    for n in range(cr - 1, -1, -1):
        lo, hi = n, top - n
        if n < cr - 1:
            x0 = res0[at(lo), :] + up[at(lo), :] * x0
            x1 = up[at(lo), :] * x1
            y0 = up[at(hi), :] * y0
            y1 = res1[at(hi), :] + up[at(hi), :] * y1
        res0[at(lo), :] = x0
        res1[at(lo), :] = x1
        res0[at(hi), :] = y0
        res1[at(hi), :] = y1

    def right_side(R, c):
        v = vs[near_slot(R, 1, c), :]
        return (
            fs[near_slot(R, 1, c), :]
            + f_w[at(R), :] * vs[near_slot(R, 0, c), :]
            + f_e[at(R), :] * vs[near_slot(R, 2, c), :]
            + f_s[at(R), :] * south(v)
            + f_n[at(R), :] * north(v)
        )

    def particular():
        low_m, high_m = [None] * 3, [None] * 3
        for n in range(cr):
            lo, hi = n, top - n
            for c in range(3):
                a, b = right_side(lo, c), right_side(hi, c)
                if n > 0:
                    a = a + below(lo) * low_m[c]
                    b = b + above(hi) * high_m[c]
                low_m[c] = a * ip[at(lo), :]
                high_m[c] = b * ip[at(hi), :]
                part[at(lo, c), :] = low_m[c]
                part[at(hi, c), :] = high_m[c]
        for c in range(3):
            x = (low_m[c] + u_low * high_m[c]) * middle
            y = high_m[c] + u_high * x
            part[at(cr - 1, c), :] = x
            part[at(cr, c), :] = y
            for n in range(cr - 2, -1, -1):
                lo, hi = n, top - n
                x = part[at(lo, c), :] + up[at(lo), :] * x
                y = part[at(hi, c), :] + up[at(hi), :] * y
                part[at(lo, c), :] = x
                part[at(hi, c), :] = y

    def gather(src, dst, phase):
        sent = []
        for d in (2, 1, 3):
            n = phase * (nc - 1) + d - 1
            sent.append((None, remote(src, dst.at[kc], peers[d - 1], rad_send.at[n], rad_recv.at[n])))
        start(sent)
        dst[kc] = src[...]
        return sent

    def piece(source, i, number):
        return source[i, pl.ds(number * WINDOW, WINDOW), :]

    def solve(factors, source, first):
        sums = [piece(source, 0, first + 3 + c) for c in range(3)]
        fixed = [[piece(source, 0, first + c) for c in range(3)]]
        olds = [None]
        for i in range(1, nc):
            f = factors[i]
            olds.append([s * f["ih"] for s in sums])
            fixed.append([f["cf"] * piece(source, i, first + c) + f["cp"] * sums[c] for c in range(3)])
            sums = [piece(source, i, first + 3 + c) + f["e1"] * sums[c] + f["e2"] * fixed[i][c] for c in range(3)]
        for c in range(3):
            flux = None
            flux_hi[nc - 1, c] = jnp.zeros((WINDOW, LANES), F32)
            flux_lo[0, c] = jnp.zeros((WINDOW, LANES), F32)
            for i in range(nc - 1, 0, -1):
                f = factors[i]
                first_value = fixed[i][c] if flux is None else fixed[i][c] + f["f1"] * flux
                last_value = olds[i][c] + f["qq"] * first_value
                flux_lo[i, c] = f["fb"] * last_value + f["dl"] * first_value
                flux = f["fb"] * first_value - f["dl"] * last_value
                flux_hi[i - 1, c] = flux

    def solved(R, c):
        return part[at(R, c), :] + res0[at(R), :] * flux_lo[kc, c] + res1[at(R), :] * flux_hi[kc, c]

    particular()
    for number, value in enumerate(
        [res0[at(0), :], res1[at(0), :], res1[at(top), :], v_at[0], v_at[top]]
        + [part[at(0, c), :] for c in range(3)]
        + [part[at(top, c), :] for c in range(3)]
    ):
        snd1[pl.ds(number * WINDOW, WINDOW), :] = value
    sent = gather(snd1, rcv1, 0)
    copies += sent

    for c in range(2):
        for R in range(rows_all):
            fin[pl.ds((c * rows_all + R) * WINDOW, WINDOW), :] = mix[near_slot(R, 1, c), :]

    def give(n, fields, first):
        made = []
        for c in range(fields):
            theirs = pl.ds(pl.multiple_of(((first + c) * rows_all + (1 - par) * cr) * WINDOW, 8), cr * WINDOW)
            made.append(to_partner(fin.at[theirs], ret.at[first + c, pl.ds(0, cr * WINDOW)], n + c))
        start(made)
        return made

    shared = give(5, 2, 0)
    for copy in shared:
        copy[1].wait_recv()
    copies += shared

    def collect(field, store):
        for i in range(1, 1 + cx // 2):
            mine = fin[pl.ds((field * rows_all + par * cr) * WINDOW + i, cr, stride=WINDOW), :]
            theirs = ret[field, pl.ds(i, cr, stride=WINDOW), :]
            store(par * (cx // 2) + i - 1, mine)
            store((1 - par) * (cx // 2) + i - 1, theirs)

    for c in range(2):
        collect(c, lambda x, value: comp.__setitem__((pl.ds(x * 2 * cr + c, cr, stride=2), slice(None)), value))
    for copy in sent:
        copy[1].wait_recv()

    factors = [None]
    slope = piece(rcv1, 0, 2)
    for i in range(1, nc):
        a, b, d, v_first = (piece(rcv1, i, n) for n in (0, 1, 2, 3))
        v_last = piece(rcv1, i - 1, 4)
        fb = 0.5 * RADIAL * (v_last + v_first)
        dl = 0.5 * RADIAL * (v_first - v_last)
        afb = a * fb
        h = 1.0 + slope * dl
        inverse_h = 1.0 / h
        inverse = 1.0 / (h * (1.0 - a * dl) - afb * (fb * slope))
        qq = fb * slope * inverse_h
        cf = h * inverse
        f1 = cf * b
        e2 = b * (fb * qq + dl)
        factors.append(dict(fb=fb, dl=dl, ih=inverse_h, qq=qq, cf=cf, cp=afb * inverse, f1=f1, e1=b * fb * inverse_h, e2=e2))
        slope = d + e2 * f1
    solve(factors, rcv1, 5)
    for c in range(3):
        for R in range(rows_all):
            vs[near_slot(R, 1, c), :] = jnp.where(inside_here, solved(R, c), 0.0)

    particular()
    for c in range(3):
        snd2[pl.ds(c * WINDOW, WINDOW), :] = part[at(0, c), :]
        snd2[pl.ds((3 + c) * WINDOW, WINDOW), :] = part[at(top, c), :]
    sent = gather(snd2, rcv2, 1)
    for copy in sent:
        copy[1].wait_recv()
    copies += sent
    solve(factors, rcv2, 0)
    for c in range(3):
        for R in range(rows_all):
            fin[pl.ds(((2 + c) * rows_all + R) * WINDOW, WINDOW), :] = solved(R, c)
    shared = give(7, 3, 2)
    for copy in shared:
        copy[1].wait_recv()
    copies += shared
    for c in range(3):
        collect(2 + c, lambda x, value: out.__setitem__((c, x), value))
    for condition, copy in copies:
        if condition is None:
            copy.wait_send()
        else:
            pl.when(condition)(copy.wait_send)


def solution(mesh):
    nl, nk = mesh.shape["lat"], mesh.shape["rad"]

    def local(tracer_values, tracer_cell, tracer_count, base_viscosity, velocity, forcing):
        cx, cr, ny = base_viscosity.shape
        slots = tracer_cell.shape[2]
        assert nk == 8 and cx + 2 * HALO == SLOTS and ny == LANES and cr == 12
        total_rows = slots // LANES
        vmem = functools.partial(pltpu.VMEM, dtype=F32)
        field = 2 * cr * SLOTS
        compact = 2 * cr * WINDOW
        spare = 8 * SLOTS
        nc = nk // 2
        scratch = [
            vmem((3 * total_rows, LANES)), vmem((total_rows, LANES)), vmem((total_rows, LANES)),
            vmem((3 * (cr // 2) * SLOTS, 2 * LANES)), vmem((2, 96, LANES)), vmem((96, LANES)), vmem((96, LANES)),
            vmem((2, 96, LANES)), vmem((2, 96, LANES)), vmem((96, LANES)), vmem((3 * (cr // 2) * SLOTS, 2 * LANES)),
            vmem((2, 3, HALO, cr, LANES)), vmem((2, 3, 1, cr, LANES)), vmem((2, HALO, cr, LANES)),
            vmem((3, cx, cr, LANES)), vmem((3, cx, cr, LANES)), vmem((cx, cr, LANES)),
            vmem((3 * field + 2 * spare, LANES)), vmem((3 * field + spare, LANES)), vmem((3 * field + spare, LANES)),
            vmem((field + spare, LANES)), vmem((field, LANES)),
        ]
        scratch += [vmem((compact, LANES))] * 8 + [vmem((3 * compact, LANES)), vmem((2 * field, LANES))]
        scratch += [vmem((Q1, LANES)), vmem((nc, Q1, LANES)), vmem((Q2, LANES)), vmem((nc, Q2, LANES))]
        scratch += [vmem((nc, 3, WINDOW, LANES))] * 2 + [vmem((compact + WINDOW, LANES))]
        scratch += [vmem((5 * compact + spare, LANES)), vmem((5, cr * WINDOW + 8 * WINDOW, LANES))]
        scratch += [pltpu.SemaphoreType.DMA((n,)) for n in (10, 10, 10, 10, 2 * (nc - 1), 2 * (nc - 1))]
        v = pl.BlockSpec(memory_space=pltpu.VMEM)
        smoothed, composition = pl.pallas_call(
            functools.partial(kernel, nl, nk),
            out_shape=[
                jax.ShapeDtypeStruct((3, cx, cr, ny), F32),
                jax.ShapeDtypeStruct((cx * cr * 2, ny), F32),
            ],
            in_specs=[v, v, pl.BlockSpec(memory_space=pltpu.SMEM), v, v, v],
            out_specs=[v, v],
            scratch_shapes=scratch,
            compiler_params=pltpu.CompilerParams(collective_id=0, has_side_effects=True),
        )(
            tracer_values.reshape(3 * total_rows, LANES),
            tracer_cell.reshape(total_rows, LANES),
            tracer_count,
            base_viscosity,
            velocity,
            forcing,
        )
        return smoothed, jnp.transpose(composition.reshape(cx, cr, 2, ny), (2, 0, 1, 3))

    return jax.shard_map(
        local,
        mesh=mesh,
        in_specs=(
            P("lat", "rad", None, None),
            P("lat", "rad", None),
            P("lat", "rad", None),
            P("lat", "rad", None),
            P(None, "lat", "rad", None),
            P(None, "lat", "rad", None),
        ),
        out_specs=(P(None, "lat", "rad", None), P(None, "lat", "rad", None)),
        check_vma=False,
    )
```

```python
import functools

import jax
import jax.numpy as jnp
from jax import lax
from jax.experimental import pallas as pl
from jax.experimental.pallas import tpu as pltpu
from jax.sharding import PartitionSpec as P

MESH = pl.DeviceIdType.MESH
F32 = jnp.float32
BF16 = jnp.bfloat16

SWEEPS = 2
LATERAL = 0.015625
RADIAL = 32.0
BUOYANCY = 0.1
PRIOR_WEIGHT = 0.5
CONTRAST_BASALT = 2.3
CONTRAST_MELT = 1.5

SLOTS = 16
HALO = 2
LANES = 128
WINDOW = 8
Q1 = 11 * WINDOW
Q2 = 6 * WINDOW


def side_index(cell, first_plane, cr):
    rows = (cell >> 7) - first_plane * cr
    plane = (rows >= cr).astype(jnp.int32)
    radial = rows - cr * plane
    return (plane * 2 + (radial & 1)) * (cr // 2) + (radial >> 1)


def stay_index(cell, cr):
    rows = cell >> 8
    half = cr // 2
    plane = (rows * 43691) >> 18
    return (rows - half * plane) * SLOTS + plane + HALO


def hot_masks(index, tiles):
    base = lax.broadcasted_iota(jnp.int32, (16, LANES), 0).astype(F32)
    return [index == (base + 16.0 * t).astype(BF16) for t in range(tiles)]


def bin_group(acc, loads, index_a, index_b, first_row, rows, step_rows, tiles_a, tiles_b, total_rows):
    zero = jnp.zeros((16, LANES), BF16)
    one = jnp.ones((16, LANES), BF16)

    def spread(ref, row):
        return jnp.broadcast_to(ref[pl.ds(row, 1), :], (16, LANES)).astype(BF16)

    def body(step, carry):
        left, right = [], []
        for j in range(step_rows):
            row = first_row + step * step_rows + j
            values = [spread(loads, q * total_rows + row) for q in range(3)]
            hot_a = hot_masks(spread(index_a, row), tiles_a)
            hot_b = hot_masks(spread(index_b, row), tiles_b)
            left.append(jnp.concatenate([jnp.where(h, v, zero) for v in values for h in hot_a], 0))
            right.append(jnp.concatenate([jnp.where(h, one, zero) for h in hot_b], 0))
        acc[...] += lax.dot_general(
            jnp.concatenate(left, 1),
            jnp.concatenate(right, 1),
            (((1,), (1,)), ((), ())),
            preferred_element_type=F32,
        )
        return carry

    lax.fori_loop(0, rows // step_rows, body, 0)


def kernel(
    nl, nk, vals_in, cell_in, cnt, bv_in, vel_in, frc_in, out, comp,
    vals, cell, bv, vel, frc, load_sem, loads, index_a, index_b, acc_s, acc_side, edge_lo, edge_hi, got_a, got_b, got_c, got_s,
    hv, hf, hb, pv, pf, pb,
    ext, vs, fs, bs, visc, f_w, f_e, f_s, f_n, up, ip, res0, res1, part, mix,
    snd1, rcv1, snd2, rcv2, flux_lo, flux_hi, share, fin, ret,
    lat_send, lat_recv, chip_send, chip_recv, rad_send, rad_recv,
):
    cx, cr = bv.shape[0], bv.shape[1]
    rows_all = 2 * cr
    half = cr // 2
    total_rows = cell.shape[0]
    rows = total_rows // 3
    nc = nk // 2
    l = lax.axis_index("lat")
    k = lax.axis_index("rad")
    kc = k // 2
    par = lax.rem(k, 2)
    lm = lax.rem(l + nl - 1, nl)
    lp = lax.rem(l + 1, nl)
    odd_below = (lm, 2 * kc + 1)
    even_above = (lp, 2 * kc)
    partner = (l, 2 * kc + 1 - par)
    peers = [(l, 2 * lax.rem(kc + d, nc) + par) for d in range(1, nc)]
    window = par * 6

    has_below = l > 0
    has_above = l < nl - 1
    has_beside = l != par * (nl - 1)

    loading = {}
    for g in (0, 2, 1):
        pairs = [(cell_in, cell, g * rows)] + [(vals_in, vals, q * total_rows + g * rows) for q in range(3)]
        loading[g] = [
            pltpu.make_async_copy(src.at[pl.ds(row, rows)], dst.at[pl.ds(row, rows)], load_sem.at[4 * g + n])
            for n, (src, dst, row) in enumerate(pairs)
        ]
    loading[3] = [
        pltpu.make_async_copy(src, dst, load_sem.at[12 + n])
        for n, (src, dst) in enumerate([(bv_in, bv), (vel_in, vel), (frc_in, frc)])
    ]
    for copies in loading.values():
        for copy in copies:
            copy.start()

    barrier = pltpu.get_barrier_semaphore()
    beside = lm + par * (lp - lm)
    for device in [partner] + peers:
        pl.semaphore_signal(barrier, inc=1, device_id=device, device_id_type=MESH)

    @pl.when(has_beside)
    def _():
        for p in range(2):
            pl.semaphore_signal(barrier, inc=1, device_id=(beside, 2 * kc + p), device_id_type=MESH)

    def remote(src, dst, device, send, recv):
        return pltpu.make_async_remote_copy(
            src_ref=src, dst_ref=dst, send_sem=send, recv_sem=recv, device_id=device, device_id_type=MESH
        )

    def to_lat(low, high, dst, n):
        return [
            (has_below, remote(low, dst.at[par], odd_below, lat_send.at[n], lat_recv.at[n + par])),
            (has_above, remote(high, dst.at[par], even_above, lat_send.at[n + 1], lat_recv.at[n + par])),
        ]

    def start(entries):
        for condition, copy in entries:
            if condition is None:
                copy.start()
            else:
                pl.when(condition)(copy.start)

    def from_lat(pairs):
        @pl.when(has_beside)
        def _():
            for dst, n in pairs:
                for p in range(2):
                    remote(dst.at[p], dst.at[p], partner, lat_send.at[n + p], lat_recv.at[n + p]).wait_recv()

    def to_partner(src, dst, n):
        return (None, remote(src, dst, partner, chip_send.at[n], chip_recv.at[n]))

    place = lax.broadcasted_iota(jnp.int32, (rows, LANES), 0) * LANES + lax.broadcasted_iota(
        jnp.int32, (rows, LANES), 1
    )
    step_rows = min(32, rows)
    acc_side[...] = jnp.zeros_like(acc_side)
    acc_s[...] = jnp.zeros_like(acc_s)

    def prepare(g):
        for copy in loading[g]:
            copy.wait()
        sl = pl.ds(g * rows, rows)
        weight = jnp.where(place < cnt[0, 0, g], 0.5 + vals[sl, :], 0.0)
        loads[sl, :] = weight
        loads[pl.ds(total_rows + g * rows, rows), :] = weight * vals[pl.ds(total_rows + g * rows, rows), :]
        loads[pl.ds(2 * total_rows + g * rows, rows), :] = weight * vals[pl.ds(2 * total_rows + g * rows, rows), :]
        c = cell[sl, :]
        if g == 1:
            index_a[sl, :] = stay_index(c, cr).astype(F32)
            index_b[sl, :] = (c & 255).astype(F32)
        else:
            index_a[sl, :] = side_index(c, cx - HALO if g == 0 else 0, cr).astype(F32)
            index_b[sl, :] = (c & 127).astype(F32)

    prepare(0)
    bin_group(acc_side.at[0], loads, index_a, index_b, 0, rows, step_rows, 2, 8, total_rows)

    pl.semaphore_wait(barrier, 1 + len(peers) + jnp.where(has_below, 1, 0) + jnp.where(has_above, 1, 0))
    copies = [to_partner(vel_in, pv, 0), to_partner(frc_in, pf, 1), to_partner(bv_in, pb, 2)]
    copies += to_lat(vel_in.at[:, pl.ds(0, HALO)], vel_in.at[:, pl.ds(cx - HALO, HALO)], hv, 0)
    copies += to_lat(frc_in.at[:, pl.ds(0, 1)], frc_in.at[:, pl.ds(cx - 1, 1)], hf, 2)
    copies += to_lat(bv_in.at[pl.ds(0, HALO)], bv_in.at[pl.ds(cx - HALO, HALO)], hb, 4)
    start(copies)

    prepare(2)
    bin_group(acc_side.at[1], loads, index_a, index_b, 2 * rows, rows, step_rows, 2, 8, total_rows)
    sides = to_lat(acc_side.at[0], acc_side.at[1], got_a, 6) + [to_partner(acc_side.at[1 - par], got_c, 3)]
    start(sides)
    prepare(1)
    bin_group(acc_s, loads, index_a, index_b, rows, rows, step_rows, 6, 16, total_rows)

    for q in range(3):
        for h in range(2):
            for s in range(HALO):
                row = (q * 4 + s * 2 + h) * half
                lanes = pl.ds(h * LANES, LANES)
                for p in range(half):
                    base = q * half * SLOTS + p * SLOTS
                    edge_lo[pl.ds(row + p, 1), :] = acc_s[pl.ds(base + HALO + s, 1), lanes]
                    edge_hi[pl.ds(row + p, 1), :] = acc_s[pl.ds(base + HALO + cx - HALO + s, 1), lanes]
    late = to_lat(edge_lo, edge_hi, got_b, 8) + [to_partner(acc_s, got_s, 4)]
    start(late)
    copies += sides + late

    field = rows_all * SLOTS

    def put(dst, c, parity, slot, value):
        dst[pl.ds(c * field + parity * cr * SLOTS + slot, cr, stride=SLOTS), :] = value

    near = par * (SLOTS - HALO)

    def kept(value):
        return jnp.where(has_beside, value, 0.0)

    ext[...] = jnp.zeros_like(ext)
    for copy in loading[3]:
        copy.wait()
    for n in range(3):
        copies[n][1].wait_recv()
    for x in range(cx):
        put(bs, 0, par, x + HALO, bv[x])
        put(bs, 0, 1 - par, x + HALO, pb[x])
        for c in range(3):
            put(vs, c, par, x + HALO, vel[c, x])
            put(vs, c, 1 - par, x + HALO, pv[c, x])
            put(fs, c, par, x + HALO, frc[c, x])
            put(fs, c, 1 - par, x + HALO, pf[c, x])
    from_lat([(hv, 0), (hf, 2), (hb, 4)])
    for p in range(2):
        for s in range(HALO):
            put(bs, 0, p, near + s, kept(hb[p, s]))
            for c in range(3):
                put(vs, c, p, near + s, kept(hv[p, c, s]))
        for c in range(3):
            put(fs, c, p, 1 + par * (SLOTS - 3), kept(hf[p, c, 0]))

    def put_edge(ref, block, parity, slot):
        for q in range(3):
            for h in range(2):
                for s in range(HALO):
                    value = ref[pl.ds(q * block + (s * 2 + h) * half, half), :]
                    start = q * field + (parity * cr + h) * SLOTS + slot + s
                    ext[pl.ds(start, half, stride=2 * SLOTS), :] = value

    from_lat([(got_a, 6)])
    for p in range(2):
        got_a[p] = kept(got_a[p])
        put_edge(got_a.at[p], 32, p, HALO + par * (SLOTS - 3 * HALO))
    sides[2][1].wait_recv()
    from_lat([(got_b, 8)])
    for q in range(3):
        theirs, mine = pl.ds(q * 4 * half, 4 * half), pl.ds(q * 32, 4 * half)
        got_b[par, theirs] = kept(got_b[par, theirs]) + acc_side[par, mine]
        got_b[1 - par, theirs] = kept(got_b[1 - par, theirs]) + got_c[mine]
    for p in range(2):
        put_edge(got_b.at[p], 4 * half, p, near)
    late[2][1].wait_recv()

    slot_of = lax.broadcasted_iota(jnp.int32, (SLOTS, LANES), 0)
    lane = lax.broadcasted_iota(jnp.int32, (WINDOW, LANES), 1)
    low = jnp.where(l == 0, HALO, 0)
    high = jnp.where(l == nl - 1, SLOTS - HALO, SLOTS)
    inside = (slot_of >= low) & (slot_of < high)
    slot_here = lax.broadcasted_iota(jnp.int32, (WINDOW, LANES), 0) + window + 1
    inside_here = (slot_here >= low) & (slot_here < high)
    is_south = lane == 0
    is_north = lane == LANES - 1

    def by_slot(R, c=0):
        return pl.ds((c * rows_all + R) * SLOTS, SLOTS)

    def near_slot(R, shift, c=0):
        return pl.ds((c * rows_all + R) * SLOTS + window + shift, WINDOW)

    def at(R, c=0):
        return pl.ds((c * rows_all + R) * WINDOW, WINDOW)

    def south(v):
        return jnp.where(is_south, 0.0, pltpu.roll(v, 1, 1))

    def north(v):
        return jnp.where(is_north, 0.0, pltpu.roll(v, LANES - 1, 1))

    for whose, ref in ((par, acc_s), (1 - par, got_s)):
        for r in range(cr):
            lanes = pl.ds((r & 1) * LANES, LANES)
            sums = []
            for q in range(3):
                more = ext[pl.ds(pl.multiple_of(q * field + (whose * cr + r) * SLOTS, 8), SLOTS), :]
                sums.append(ref[pl.ds((q * half + r // 2) * SLOTS, SLOTS), lanes] + more)
            inverse = 1.0 / (sums[0] + PRIOR_WEIGHT)
            basalt = sums[1] * inverse
            melt = sums[2] * inverse
            here = pl.ds(pl.multiple_of((whose * cr + r) * SLOTS, 8), SLOTS)
            mix[here, :] = basalt
            mix[pl.ds(pl.multiple_of(field + (whose * cr + r) * SLOTS, 8), SLOTS), :] = melt
            heavy = pl.ds(pl.multiple_of(2 * field + (whose * cr + r) * SLOTS, 8), SLOTS)
            fs[heavy, :] = fs[heavy, :] - BUOYANCY * basalt
            visc[here, :] = jnp.where(
                inside, bs[here, :] * jnp.exp(CONTRAST_BASALT * basalt - CONTRAST_MELT * melt), 0.0
            )

    weight_lo = jnp.where(kc == 0, 0.5 * RADIAL, RADIAL)
    weight_hi = jnp.where(kc == nc - 1, 0.5 * RADIAL, RADIAL)
    top = rows_all - 1
    v_at = [visc[near_slot(R, 1), :] for R in range(rows_all)]
    face = [weight_lo * v_at[0]]
    face += [0.5 * RADIAL * (v_at[R - 1] + v_at[R]) for R in range(1, rows_all)]
    face += [weight_hi * v_at[top]]
    face_ref = share
    for R in range(rows_all + 1):
        face_ref[pl.ds(R * WINDOW, WINDOW), :] = face[R]

    def below(R):
        return face_ref[pl.ds(R * WINDOW, WINDOW), :]

    def above(R):
        return below(R + 1)

    def diagonal(R):
        v = visc[near_slot(R, 1), :]
        scale = LATERAL * 0.5
        fw = scale * (v + visc[near_slot(R, 0), :])
        fe = scale * (v + visc[near_slot(R, 2), :])
        fs_, fn = scale * (v + south(v)), scale * (v + north(v))
        f_w[at(R), :] = fw
        f_e[at(R), :] = fe
        f_s[at(R), :] = fs_
        f_n[at(R), :] = fn
        return jnp.where(v > 0.0, fw + fe + fs_ + fn + below(R) + above(R), 1.0)

    u_low = u_high = m_low = m_high = None
    for n in range(cr):
        lo, hi = n, top - n
        p_low, p_high = diagonal(lo), diagonal(hi)
        if n > 0:
            p_low = p_low - below(lo) * u_low
            p_high = p_high - above(hi) * u_high
        i_low, i_high = 1.0 / p_low, 1.0 / p_high
        ip[at(lo), :] = i_low
        ip[at(hi), :] = i_high
        m_low = i_low if n == 0 else below(lo) * m_low * i_low
        m_high = i_high if n == 0 else above(hi) * m_high * i_high
        res0[at(lo), :] = m_low
        res1[at(hi), :] = m_high
        u_low, u_high = above(lo) * i_low, below(hi) * i_high
        up[at(lo), :] = u_low
        up[at(hi), :] = u_high
    middle = 1.0 / (1.0 - u_low * u_high)

    x0, y1 = m_low * middle, m_high * middle
    y0, x1 = u_high * x0, u_low * y1
    for n in range(cr - 1, -1, -1):
        lo, hi = n, top - n
        if n < cr - 1:
            x0 = res0[at(lo), :] + up[at(lo), :] * x0
            x1 = up[at(lo), :] * x1
            y0 = up[at(hi), :] * y0
            y1 = res1[at(hi), :] + up[at(hi), :] * y1
        res0[at(lo), :] = x0
        res1[at(lo), :] = x1
        res0[at(hi), :] = y0
        res1[at(hi), :] = y1

    def right_side(R, c):
        v = vs[near_slot(R, 1, c), :]
        return (
            fs[near_slot(R, 1, c), :]
            + f_w[at(R), :] * vs[near_slot(R, 0, c), :]
            + f_e[at(R), :] * vs[near_slot(R, 2, c), :]
            + f_s[at(R), :] * south(v)
            + f_n[at(R), :] * north(v)
        )

    def particular():
        low_m, high_m = [None] * 3, [None] * 3
        for n in range(cr):
            lo, hi = n, top - n
            for c in range(3):
                a, b = right_side(lo, c), right_side(hi, c)
                if n > 0:
                    a = a + below(lo) * low_m[c]
                    b = b + above(hi) * high_m[c]
                low_m[c] = a * ip[at(lo), :]
                high_m[c] = b * ip[at(hi), :]
                part[at(lo, c), :] = low_m[c]
                part[at(hi, c), :] = high_m[c]
        for c in range(3):
            x = (low_m[c] + u_low * high_m[c]) * middle
            y = high_m[c] + u_high * x
            part[at(cr - 1, c), :] = x
            part[at(cr, c), :] = y
            for n in range(cr - 2, -1, -1):
                lo, hi = n, top - n
                x = part[at(lo, c), :] + up[at(lo), :] * x
                y = part[at(hi, c), :] + up[at(hi), :] * y
                part[at(lo, c), :] = x
                part[at(hi, c), :] = y

    def gather(src, dst, phase):
        sent = []
        for d in (2, 1, 3):
            n = phase * (nc - 1) + d - 1
            sent.append((None, remote(src, dst.at[kc], peers[d - 1], rad_send.at[n], rad_recv.at[n])))
        start(sent)
        dst[kc] = src[...]
        return sent

    def piece(source, i, number):
        return source[i, pl.ds(number * WINDOW, WINDOW), :]

    def solve(factors, source, first):
        sums = [piece(source, 0, first + 3 + c) for c in range(3)]
        fixed = [[piece(source, 0, first + c) for c in range(3)]]
        olds = [None]
        for i in range(1, nc):
            f = factors[i]
            olds.append([s * f["ih"] for s in sums])
            fixed.append([f["cf"] * piece(source, i, first + c) + f["cp"] * sums[c] for c in range(3)])
            sums = [piece(source, i, first + 3 + c) + f["e1"] * sums[c] + f["e2"] * fixed[i][c] for c in range(3)]
        for c in range(3):
            flux = None
            flux_hi[nc - 1, c] = jnp.zeros((WINDOW, LANES), F32)
            flux_lo[0, c] = jnp.zeros((WINDOW, LANES), F32)
            for i in range(nc - 1, 0, -1):
                f = factors[i]
                first_value = fixed[i][c] if flux is None else fixed[i][c] + f["f1"] * flux
                last_value = olds[i][c] + f["qq"] * first_value
                flux_lo[i, c] = f["fb"] * last_value + f["dl"] * first_value
                flux = f["fb"] * first_value - f["dl"] * last_value
                flux_hi[i - 1, c] = flux

    def solved(R, c):
        return part[at(R, c), :] + res0[at(R), :] * flux_lo[kc, c] + res1[at(R), :] * flux_hi[kc, c]

    particular()
    for number, value in enumerate(
        [res0[at(0), :], res1[at(0), :], res1[at(top), :], v_at[0], v_at[top]]
        + [part[at(0, c), :] for c in range(3)]
        + [part[at(top, c), :] for c in range(3)]
    ):
        snd1[pl.ds(number * WINDOW, WINDOW), :] = value
    sent = gather(snd1, rcv1, 0)
    copies += sent

    for c in range(2):
        for R in range(rows_all):
            fin[pl.ds((c * rows_all + R) * WINDOW, WINDOW), :] = mix[near_slot(R, 1, c), :]

    def give(n, fields, first):
        made = []
        for c in range(fields):
            theirs = pl.ds(pl.multiple_of(((first + c) * rows_all + (1 - par) * cr) * WINDOW, 8), cr * WINDOW)
            made.append(to_partner(fin.at[theirs], ret.at[first + c, pl.ds(0, cr * WINDOW)], n + c))
        start(made)
        return made

    shared = give(5, 2, 0)
    for copy in shared:
        copy[1].wait_recv()
    copies += shared

    def collect(field, store):
        for i in range(1, 1 + cx // 2):
            mine = fin[pl.ds((field * rows_all + par * cr) * WINDOW + i, cr, stride=WINDOW), :]
            theirs = ret[field, pl.ds(i, cr, stride=WINDOW), :]
            store(par * (cx // 2) + i - 1, mine)
            store((1 - par) * (cx // 2) + i - 1, theirs)

    for c in range(2):
        collect(c, lambda x, value: comp.__setitem__((pl.ds(x * 2 * cr + c, cr, stride=2), slice(None)), value))
    for copy in sent:
        copy[1].wait_recv()

    factors = [None]
    slope = piece(rcv1, 0, 2)
    for i in range(1, nc):
        a, b, d, v_first = (piece(rcv1, i, n) for n in (0, 1, 2, 3))
        v_last = piece(rcv1, i - 1, 4)
        fb = 0.5 * RADIAL * (v_last + v_first)
        dl = 0.5 * RADIAL * (v_first - v_last)
        afb = a * fb
        h = 1.0 + slope * dl
        inverse_h = 1.0 / h
        inverse = 1.0 / (h * (1.0 - a * dl) - afb * (fb * slope))
        qq = fb * slope * inverse_h
        cf = h * inverse
        f1 = cf * b
        e2 = b * (fb * qq + dl)
        factors.append(dict(fb=fb, dl=dl, ih=inverse_h, qq=qq, cf=cf, cp=afb * inverse, f1=f1, e1=b * fb * inverse_h, e2=e2))
        slope = d + e2 * f1
    solve(factors, rcv1, 5)
    for c in range(3):
        for R in range(rows_all):
            vs[near_slot(R, 1, c), :] = jnp.where(inside_here, solved(R, c), 0.0)

    particular()
    for c in range(3):
        snd2[pl.ds(c * WINDOW, WINDOW), :] = part[at(0, c), :]
        snd2[pl.ds((3 + c) * WINDOW, WINDOW), :] = part[at(top, c), :]
    sent = gather(snd2, rcv2, 1)
    for copy in sent:
        copy[1].wait_recv()
    copies += sent
    solve(factors, rcv2, 0)
    for c in range(3):
        for R in range(rows_all):
            fin[pl.ds(((2 + c) * rows_all + R) * WINDOW, WINDOW), :] = solved(R, c)
    shared = give(7, 3, 2)
    for copy in shared:
        copy[1].wait_recv()
    copies += shared
    for c in range(3):
        collect(2 + c, lambda x, value: out.__setitem__((c, x), value))
    for condition, copy in copies:
        if condition is None:
            copy.wait_send()
        else:
            pl.when(condition)(copy.wait_send)


def solution(mesh):
    nl, nk = mesh.shape["lat"], mesh.shape["rad"]

    def local(tracer_values, tracer_cell, tracer_count, base_viscosity, velocity, forcing):
        cx, cr, ny = base_viscosity.shape
        slots = tracer_cell.shape[2]
        assert nk == 8 and cx + 2 * HALO == SLOTS and ny == LANES and cr == 12
        total_rows = slots // LANES
        vmem = functools.partial(pltpu.VMEM, dtype=F32)
        field = 2 * cr * SLOTS
        compact = 2 * cr * WINDOW
        spare = 8 * SLOTS
        nc = nk // 2
        scratch = [
            vmem((3 * total_rows, LANES)), pltpu.VMEM((total_rows, LANES), jnp.int32), vmem((cx, cr, LANES)),
            vmem((3, cx, cr, LANES)), vmem((3, cx, cr, LANES)), pltpu.SemaphoreType.DMA((15,)),
            vmem((3 * total_rows, LANES)), vmem((total_rows, LANES)), vmem((total_rows, LANES)),
            vmem((3 * (cr // 2) * SLOTS, 2 * LANES)), vmem((2, 96, LANES)), vmem((72, LANES)), vmem((72, LANES)),
            vmem((2, 96, LANES)), vmem((2, 72, LANES)), vmem((96, LANES)), vmem((3 * (cr // 2) * SLOTS, 2 * LANES)),
            vmem((2, 3, HALO, cr, LANES)), vmem((2, 3, 1, cr, LANES)), vmem((2, HALO, cr, LANES)),
            vmem((3, cx, cr, LANES)), vmem((3, cx, cr, LANES)), vmem((cx, cr, LANES)),
            vmem((3 * field + 2 * spare, LANES)), vmem((3 * field + spare, LANES)), vmem((3 * field + spare, LANES)),
            vmem((field + spare, LANES)), vmem((field, LANES)),
        ]
        scratch += [vmem((compact, LANES))] * 8 + [vmem((3 * compact, LANES)), vmem((2 * field, LANES))]
        scratch += [vmem((Q1, LANES)), vmem((nc, Q1, LANES)), vmem((Q2, LANES)), vmem((nc, Q2, LANES))]
        scratch += [vmem((nc, 3, WINDOW, LANES))] * 2 + [vmem((compact + WINDOW, LANES))]
        scratch += [vmem((5 * compact + spare, LANES)), vmem((5, cr * WINDOW + 8 * WINDOW, LANES))]
        scratch += [pltpu.SemaphoreType.DMA((n,)) for n in (10, 10, 10, 10, 2 * (nc - 1), 2 * (nc - 1))]
        v = pl.BlockSpec(memory_space=pltpu.VMEM)
        h = pl.BlockSpec(memory_space=pltpu.HBM)
        smoothed, composition = pl.pallas_call(
            functools.partial(kernel, nl, nk),
            out_shape=[
                pltpu.VMEM((3, cx, cr, ny), F32),
                pltpu.VMEM((cx * cr * 2, ny), F32),
            ],
            in_specs=[h, h, pl.BlockSpec(memory_space=pltpu.SMEM), h, h, h],
            out_specs=[v, v],
            scratch_shapes=scratch,
            compiler_params=pltpu.CompilerParams(collective_id=0, has_side_effects=True),
        )(
            tracer_values.reshape(3 * total_rows, LANES),
            tracer_cell.reshape(total_rows, LANES),
            tracer_count,
            base_viscosity,
            velocity,
            forcing,
        )
        return smoothed, jnp.transpose(composition.reshape(cx, cr, 2, ny), (2, 0, 1, 3))

    return jax.shard_map(
        local,
        mesh=mesh,
        in_specs=(
            P("lat", "rad", None, None),
            P("lat", "rad", None),
            P("lat", "rad", None),
            P("lat", "rad", None),
            P(None, "lat", "rad", None),
            P(None, "lat", "rad", None),
        ),
        out_specs=(P(None, "lat", "rad", None), P(None, "lat", "rad", None)),
        check_vma=False,
    )
```

```python
import functools

import jax
import jax.numpy as jnp
from jax import lax
from jax.experimental import pallas as pl
from jax.experimental.pallas import tpu as pltpu
from jax.sharding import PartitionSpec as P

MESH = pl.DeviceIdType.MESH
F32 = jnp.float32
BF16 = jnp.bfloat16

SWEEPS = 2
LATERAL = 0.015625
RADIAL = 32.0
BUOYANCY = 0.1
PRIOR_WEIGHT = 0.5
CONTRAST_BASALT = 2.3
CONTRAST_MELT = 1.5

SLOTS = 16
HALO = 2
LANES = 128
WINDOW = 8
Q1 = 11 * WINDOW
Q2 = 6 * WINDOW


def side_index(cell, first_plane, cr):
    rows = (cell >> 7) - first_plane * cr
    plane = (rows >= cr).astype(jnp.int32)
    radial = rows - cr * plane
    return (plane * 2 + (radial & 1)) * (cr // 2) + (radial >> 1)


def stay_index(cell, cr):
    rows = cell >> 8
    half = cr // 2
    plane = (rows * 43691) >> 18
    return (rows - half * plane) * SLOTS + plane + HALO


def hot_masks(index, tiles):
    base = lax.broadcasted_iota(jnp.int32, (16, LANES), 0).astype(F32)
    return [index == (base + 16.0 * t).astype(BF16) for t in range(tiles)]


def bin_group(acc, loads, index_a, index_b, first_row, rows, step_rows, tiles_a, tiles_b, total_rows):
    zero = jnp.zeros((16, LANES), BF16)
    one = jnp.ones((16, LANES), BF16)

    def spread(ref, row):
        return jnp.broadcast_to(ref[pl.ds(row, 1), :], (16, LANES)).astype(BF16)

    def body(step, carry):
        left, right = [], []
        for j in range(step_rows):
            row = first_row + step * step_rows + j
            values = [spread(loads, q * total_rows + row) for q in range(3)]
            hot_a = hot_masks(spread(index_a, row), tiles_a)
            hot_b = hot_masks(spread(index_b, row), tiles_b)
            left.append(jnp.concatenate([jnp.where(h, v, zero) for v in values for h in hot_a], 0))
            right.append(jnp.concatenate([jnp.where(h, one, zero) for h in hot_b], 0))
        acc[...] += lax.dot_general(
            jnp.concatenate(left, 1),
            jnp.concatenate(right, 1),
            (((1,), (1,)), ((), ())),
            preferred_element_type=F32,
        )
        return carry

    lax.fori_loop(0, rows // step_rows, body, 0)


def kernel(
    nl, nk, vals_in, cell_in, cnt_in, bv_in, vel_in, frc_in, out, comp,
    cnt, vals, cell, bv, vel, frc, load_sem, loads, index_a, index_b, acc_s, acc_side, edge_lo, edge_hi, got_a, got_b, got_c, got_s,
    hv, hf, hb, pv, pf, pb,
    ext, vs, fs, bs, visc, f_w, f_e, f_s, f_n, up, ip, res0, res1, part, mix,
    snd1, rcv1, snd2, rcv2, flux_lo, flux_hi, share, fin, ret,
    lat_send, lat_recv, chip_send, chip_recv, rad_send, rad_recv,
):
    cx, cr = bv.shape[0], bv.shape[1]
    rows_all = 2 * cr
    half = cr // 2
    total_rows = cell.shape[0]
    rows = total_rows // 3
    nc = nk // 2
    l = lax.axis_index("lat")
    k = lax.axis_index("rad")
    kc = k // 2
    par = lax.rem(k, 2)
    lm = lax.rem(l + nl - 1, nl)
    lp = lax.rem(l + 1, nl)
    odd_below = (lm, 2 * kc + 1)
    even_above = (lp, 2 * kc)
    partner = (l, 2 * kc + 1 - par)
    peers = [(l, 2 * lax.rem(kc + d, nc) + par) for d in range(1, nc)]
    window = par * 6

    has_below = l > 0
    has_above = l < nl - 1
    has_beside = l != par * (nl - 1)

    loading = {4: [pltpu.make_async_copy(cnt_in, cnt, load_sem.at[15])]}
    for g in (0, 2, 1):
        pairs = [(cell_in, cell, g * rows)] + [(vals_in, vals, q * total_rows + g * rows) for q in range(3)]
        loading[g] = [
            pltpu.make_async_copy(src.at[pl.ds(row, rows)], dst.at[pl.ds(row, rows)], load_sem.at[4 * g + n])
            for n, (src, dst, row) in enumerate(pairs)
        ]
    loading[3] = [
        pltpu.make_async_copy(src, dst, load_sem.at[12 + n])
        for n, (src, dst) in enumerate([(bv_in, bv), (vel_in, vel), (frc_in, frc)])
    ]
    for copies in loading.values():
        for copy in copies:
            copy.start()

    barrier = pltpu.get_barrier_semaphore()
    beside = lm + par * (lp - lm)
    for device in [partner] + peers:
        pl.semaphore_signal(barrier, inc=1, device_id=device, device_id_type=MESH)

    @pl.when(has_beside)
    def _():
        for p in range(2):
            pl.semaphore_signal(barrier, inc=1, device_id=(beside, 2 * kc + p), device_id_type=MESH)

    def remote(src, dst, device, send, recv):
        return pltpu.make_async_remote_copy(
            src_ref=src, dst_ref=dst, send_sem=send, recv_sem=recv, device_id=device, device_id_type=MESH
        )

    def to_lat(low, high, dst, n):
        return [
            (has_below, remote(low, dst.at[par], odd_below, lat_send.at[n], lat_recv.at[n + par])),
            (has_above, remote(high, dst.at[par], even_above, lat_send.at[n + 1], lat_recv.at[n + par])),
        ]

    def start(entries):
        for condition, copy in entries:
            if condition is None:
                copy.start()
            else:
                pl.when(condition)(copy.start)

    def from_lat(pairs):
        @pl.when(has_beside)
        def _():
            for dst, n in pairs:
                for p in range(2):
                    remote(dst.at[p], dst.at[p], partner, lat_send.at[n + p], lat_recv.at[n + p]).wait_recv()

    def to_partner(src, dst, n):
        return (None, remote(src, dst, partner, chip_send.at[n], chip_recv.at[n]))

    place = lax.broadcasted_iota(jnp.int32, (rows, LANES), 0) * LANES + lax.broadcasted_iota(
        jnp.int32, (rows, LANES), 1
    )
    step_rows = min(32, rows)
    acc_side[...] = jnp.zeros_like(acc_side)
    acc_s[...] = jnp.zeros_like(acc_s)

    def prepare(g):
        for copy in loading[g]:
            copy.wait()
        sl = pl.ds(g * rows, rows)
        weight = jnp.where(place < cnt[0, 0, g], 0.5 + vals[sl, :], 0.0)
        loads[sl, :] = weight
        loads[pl.ds(total_rows + g * rows, rows), :] = weight * vals[pl.ds(total_rows + g * rows, rows), :]
        loads[pl.ds(2 * total_rows + g * rows, rows), :] = weight * vals[pl.ds(2 * total_rows + g * rows, rows), :]
        c = cell[sl, :]
        if g == 1:
            index_a[sl, :] = stay_index(c, cr).astype(F32)
            index_b[sl, :] = (c & 255).astype(F32)
        else:
            index_a[sl, :] = side_index(c, cx - HALO if g == 0 else 0, cr).astype(F32)
            index_b[sl, :] = (c & 127).astype(F32)

    loading[4][0].wait()
    prepare(0)
    bin_group(acc_side.at[0], loads, index_a, index_b, 0, rows, step_rows, 2, 8, total_rows)

    pl.semaphore_wait(barrier, 1 + len(peers) + jnp.where(has_below, 1, 0) + jnp.where(has_above, 1, 0))
    copies = [to_partner(vel_in, pv, 0), to_partner(frc_in, pf, 1), to_partner(bv_in, pb, 2)]
    copies += to_lat(vel_in.at[:, pl.ds(0, HALO)], vel_in.at[:, pl.ds(cx - HALO, HALO)], hv, 0)
    copies += to_lat(frc_in.at[:, pl.ds(0, 1)], frc_in.at[:, pl.ds(cx - 1, 1)], hf, 2)
    copies += to_lat(bv_in.at[pl.ds(0, HALO)], bv_in.at[pl.ds(cx - HALO, HALO)], hb, 4)
    start(copies)

    prepare(2)
    bin_group(acc_side.at[1], loads, index_a, index_b, 2 * rows, rows, step_rows, 2, 8, total_rows)
    sides = to_lat(acc_side.at[0], acc_side.at[1], got_a, 6) + [to_partner(acc_side.at[1 - par], got_c, 3)]
    start(sides)
    prepare(1)
    bin_group(acc_s, loads, index_a, index_b, rows, rows, min(64, rows), 6, 16, total_rows)

    for q in range(3):
        for h in range(2):
            for s in range(HALO):
                row = (q * 4 + s * 2 + h) * half
                lanes = pl.ds(h * LANES, LANES)
                for p in range(half):
                    base = q * half * SLOTS + p * SLOTS
                    edge_lo[pl.ds(row + p, 1), :] = acc_s[pl.ds(base + HALO + s, 1), lanes]
                    edge_hi[pl.ds(row + p, 1), :] = acc_s[pl.ds(base + HALO + cx - HALO + s, 1), lanes]
    late = to_lat(edge_lo, edge_hi, got_b, 8) + [to_partner(acc_s, got_s, 4)]
    start(late)
    copies += sides + late

    field = rows_all * SLOTS

    def put(dst, c, parity, slot, value):
        dst[pl.ds(c * field + parity * cr * SLOTS + slot, cr, stride=SLOTS), :] = value

    near = par * (SLOTS - HALO)

    def kept(value):
        return jnp.where(has_beside, value, 0.0)

    ext[...] = jnp.zeros_like(ext)
    for copy in loading[3]:
        copy.wait()
    for n in range(3):
        copies[n][1].wait_recv()
    for x in range(cx):
        put(bs, 0, par, x + HALO, bv[x])
        put(bs, 0, 1 - par, x + HALO, pb[x])
        for c in range(3):
            put(vs, c, par, x + HALO, vel[c, x])
            put(vs, c, 1 - par, x + HALO, pv[c, x])
            put(fs, c, par, x + HALO, frc[c, x])
            put(fs, c, 1 - par, x + HALO, pf[c, x])
    from_lat([(hv, 0), (hf, 2), (hb, 4)])
    for p in range(2):
        for s in range(HALO):
            put(bs, 0, p, near + s, kept(hb[p, s]))
            for c in range(3):
                put(vs, c, p, near + s, kept(hv[p, c, s]))
        for c in range(3):
            put(fs, c, p, 1 + par * (SLOTS - 3), kept(hf[p, c, 0]))

    def put_edge(ref, block, parity, slot):
        for q in range(3):
            for h in range(2):
                for s in range(HALO):
                    value = ref[pl.ds(q * block + (s * 2 + h) * half, half), :]
                    start = q * field + (parity * cr + h) * SLOTS + slot + s
                    ext[pl.ds(start, half, stride=2 * SLOTS), :] = value

    from_lat([(got_a, 6)])
    for p in range(2):
        got_a[p] = kept(got_a[p])
        put_edge(got_a.at[p], 32, p, HALO + par * (SLOTS - 3 * HALO))
    sides[2][1].wait_recv()
    from_lat([(got_b, 8)])
    for q in range(3):
        theirs, mine = pl.ds(q * 4 * half, 4 * half), pl.ds(q * 32, 4 * half)
        got_b[par, theirs] = kept(got_b[par, theirs]) + acc_side[par, mine]
        got_b[1 - par, theirs] = kept(got_b[1 - par, theirs]) + got_c[mine]
    for p in range(2):
        put_edge(got_b.at[p], 4 * half, p, near)
    late[2][1].wait_recv()

    slot_of = lax.broadcasted_iota(jnp.int32, (SLOTS, LANES), 0)
    lane = lax.broadcasted_iota(jnp.int32, (WINDOW, LANES), 1)
    low = jnp.where(l == 0, HALO, 0)
    high = jnp.where(l == nl - 1, SLOTS - HALO, SLOTS)
    inside = (slot_of >= low) & (slot_of < high)
    slot_here = lax.broadcasted_iota(jnp.int32, (WINDOW, LANES), 0) + window + 1
    inside_here = (slot_here >= low) & (slot_here < high)
    is_south = lane == 0
    is_north = lane == LANES - 1

    def by_slot(R, c=0):
        return pl.ds((c * rows_all + R) * SLOTS, SLOTS)

    def near_slot(R, shift, c=0):
        return pl.ds((c * rows_all + R) * SLOTS + window + shift, WINDOW)

    def at(R, c=0):
        return pl.ds((c * rows_all + R) * WINDOW, WINDOW)

    def south(v):
        return jnp.where(is_south, 0.0, pltpu.roll(v, 1, 1))

    def north(v):
        return jnp.where(is_north, 0.0, pltpu.roll(v, LANES - 1, 1))

    for whose, ref in ((par, acc_s), (1 - par, got_s)):
        for r in range(cr):
            lanes = pl.ds((r & 1) * LANES, LANES)
            sums = []
            for q in range(3):
                more = ext[pl.ds(pl.multiple_of(q * field + (whose * cr + r) * SLOTS, 8), SLOTS), :]
                sums.append(ref[pl.ds((q * half + r // 2) * SLOTS, SLOTS), lanes] + more)
            inverse = 1.0 / (sums[0] + PRIOR_WEIGHT)
            basalt = sums[1] * inverse
            melt = sums[2] * inverse
            here = pl.ds(pl.multiple_of((whose * cr + r) * SLOTS, 8), SLOTS)
            mix[here, :] = basalt
            mix[pl.ds(pl.multiple_of(field + (whose * cr + r) * SLOTS, 8), SLOTS), :] = melt
            heavy = pl.ds(pl.multiple_of(2 * field + (whose * cr + r) * SLOTS, 8), SLOTS)
            fs[heavy, :] = fs[heavy, :] - BUOYANCY * basalt
            visc[here, :] = jnp.where(
                inside, bs[here, :] * jnp.exp(CONTRAST_BASALT * basalt - CONTRAST_MELT * melt), 0.0
            )

    weight_lo = jnp.where(kc == 0, 0.5 * RADIAL, RADIAL)
    weight_hi = jnp.where(kc == nc - 1, 0.5 * RADIAL, RADIAL)
    top = rows_all - 1
    v_at = [visc[near_slot(R, 1), :] for R in range(rows_all)]
    face = [weight_lo * v_at[0]]
    face += [0.5 * RADIAL * (v_at[R - 1] + v_at[R]) for R in range(1, rows_all)]
    face += [weight_hi * v_at[top]]
    face_ref = share
    for R in range(rows_all + 1):
        face_ref[pl.ds(R * WINDOW, WINDOW), :] = face[R]

    def below(R):
        return face_ref[pl.ds(R * WINDOW, WINDOW), :]

    def above(R):
        return below(R + 1)

    def diagonal(R):
        v = visc[near_slot(R, 1), :]
        scale = LATERAL * 0.5
        fw = scale * (v + visc[near_slot(R, 0), :])
        fe = scale * (v + visc[near_slot(R, 2), :])
        fs_, fn = scale * (v + south(v)), scale * (v + north(v))
        f_w[at(R), :] = fw
        f_e[at(R), :] = fe
        f_s[at(R), :] = fs_
        f_n[at(R), :] = fn
        return jnp.where(v > 0.0, fw + fe + fs_ + fn + below(R) + above(R), 1.0)

    u_low = u_high = m_low = m_high = None
    for n in range(cr):
        lo, hi = n, top - n
        p_low, p_high = diagonal(lo), diagonal(hi)
        if n > 0:
            p_low = p_low - below(lo) * u_low
            p_high = p_high - above(hi) * u_high
        i_low, i_high = 1.0 / p_low, 1.0 / p_high
        ip[at(lo), :] = i_low
        ip[at(hi), :] = i_high
        m_low = i_low if n == 0 else below(lo) * m_low * i_low
        m_high = i_high if n == 0 else above(hi) * m_high * i_high
        res0[at(lo), :] = m_low
        res1[at(hi), :] = m_high
        u_low, u_high = above(lo) * i_low, below(hi) * i_high
        up[at(lo), :] = u_low
        up[at(hi), :] = u_high
    middle = 1.0 / (1.0 - u_low * u_high)

    x0, y1 = m_low * middle, m_high * middle
    y0, x1 = u_high * x0, u_low * y1
    for n in range(cr - 1, -1, -1):
        lo, hi = n, top - n
        if n < cr - 1:
            x0 = res0[at(lo), :] + up[at(lo), :] * x0
            x1 = up[at(lo), :] * x1
            y0 = up[at(hi), :] * y0
            y1 = res1[at(hi), :] + up[at(hi), :] * y1
        res0[at(lo), :] = x0
        res1[at(lo), :] = x1
        res0[at(hi), :] = y0
        res1[at(hi), :] = y1

    def right_side(R, c):
        v = vs[near_slot(R, 1, c), :]
        return (
            fs[near_slot(R, 1, c), :]
            + f_w[at(R), :] * vs[near_slot(R, 0, c), :]
            + f_e[at(R), :] * vs[near_slot(R, 2, c), :]
            + f_s[at(R), :] * south(v)
            + f_n[at(R), :] * north(v)
        )

    def particular():
        low_m, high_m = [None] * 3, [None] * 3
        for n in range(cr):
            lo, hi = n, top - n
            for c in range(3):
                a, b = right_side(lo, c), right_side(hi, c)
                if n > 0:
                    a = a + below(lo) * low_m[c]
                    b = b + above(hi) * high_m[c]
                low_m[c] = a * ip[at(lo), :]
                high_m[c] = b * ip[at(hi), :]
                part[at(lo, c), :] = low_m[c]
                part[at(hi, c), :] = high_m[c]
        for c in range(3):
            x = (low_m[c] + u_low * high_m[c]) * middle
            y = high_m[c] + u_high * x
            part[at(cr - 1, c), :] = x
            part[at(cr, c), :] = y
            for n in range(cr - 2, -1, -1):
                lo, hi = n, top - n
                x = part[at(lo, c), :] + up[at(lo), :] * x
                y = part[at(hi, c), :] + up[at(hi), :] * y
                part[at(lo, c), :] = x
                part[at(hi, c), :] = y

    def gather(src, dst, phase, where):
        sent = []
        for d in (2, 1, 3):
            n = phase * (nc - 1) + d - 1
            sent.append((None, remote(src.at[where], dst.at[kc, where], peers[d - 1], rad_send.at[n], rad_recv.at[n])))
        start(sent)
        dst[kc, where] = src[where]
        return sent

    def piece(source, i, number):
        return source[i, pl.ds(number * WINDOW, WINDOW), :]

    def solve(factors, source, first):
        sums = [piece(source, 0, first + 3 + c) for c in range(3)]
        fixed = [[piece(source, 0, first + c) for c in range(3)]]
        olds = [None]
        for i in range(1, nc):
            f = factors[i]
            olds.append([s * f["ih"] for s in sums])
            fixed.append([f["cf"] * piece(source, i, first + c) + f["cp"] * sums[c] for c in range(3)])
            sums = [piece(source, i, first + 3 + c) + f["e1"] * sums[c] + f["e2"] * fixed[i][c] for c in range(3)]
        for c in range(3):
            flux = None
            flux_hi[nc - 1, c] = jnp.zeros((WINDOW, LANES), F32)
            flux_lo[0, c] = jnp.zeros((WINDOW, LANES), F32)
            for i in range(nc - 1, 0, -1):
                f = factors[i]
                first_value = fixed[i][c] if flux is None else fixed[i][c] + f["f1"] * flux
                last_value = olds[i][c] + f["qq"] * first_value
                flux_lo[i, c] = f["fb"] * last_value + f["dl"] * first_value
                flux = f["fb"] * first_value - f["dl"] * last_value
                flux_hi[i - 1, c] = flux

    def solved(R, c):
        return part[at(R, c), :] + res0[at(R), :] * flux_lo[kc, c] + res1[at(R), :] * flux_hi[kc, c]

    for number, value in enumerate([res0[at(0), :], res1[at(0), :], res1[at(top), :], v_at[0], v_at[top]]):
        snd1[pl.ds(number * WINDOW, WINDOW), :] = value
    sent = gather(snd1, rcv1, 2, pl.ds(0, 5 * WINDOW))
    particular()
    for c in range(3):
        snd1[pl.ds((5 + c) * WINDOW, WINDOW), :] = part[at(0, c), :]
        snd1[pl.ds((8 + c) * WINDOW, WINDOW), :] = part[at(top, c), :]
    sent += gather(snd1, rcv1, 0, pl.ds(5 * WINDOW, 6 * WINDOW))
    copies += sent

    for c in range(2):
        for R in range(rows_all):
            fin[pl.ds((c * rows_all + R) * WINDOW, WINDOW), :] = mix[near_slot(R, 1, c), :]

    def give(n, fields, first):
        made = []
        for c in range(fields):
            theirs = pl.ds(pl.multiple_of(((first + c) * rows_all + (1 - par) * cr) * WINDOW, 8), cr * WINDOW)
            made.append(to_partner(fin.at[theirs], ret.at[first + c, pl.ds(0, cr * WINDOW)], n + c))
        start(made)
        return made

    shared = give(5, 2, 0)
    for copy in shared:
        copy[1].wait_recv()
    copies += shared

    def collect(field, store):
        for i in range(1, 1 + cx // 2):
            mine = fin[pl.ds((field * rows_all + par * cr) * WINDOW + i, cr, stride=WINDOW), :]
            theirs = ret[field, pl.ds(i, cr, stride=WINDOW), :]
            store(par * (cx // 2) + i - 1, mine)
            store((1 - par) * (cx // 2) + i - 1, theirs)

    for c in range(2):
        collect(c, lambda x, value: comp.__setitem__((pl.ds(x * 2 * cr + c, cr, stride=2), slice(None)), value))
    for copy in sent:
        copy[1].wait_recv()

    factors = [None]
    slope = piece(rcv1, 0, 2)
    for i in range(1, nc):
        a, b, d, v_first = (piece(rcv1, i, n) for n in (0, 1, 2, 3))
        v_last = piece(rcv1, i - 1, 4)
        fb = 0.5 * RADIAL * (v_last + v_first)
        dl = 0.5 * RADIAL * (v_first - v_last)
        afb = a * fb
        h = 1.0 + slope * dl
        inverse_h = 1.0 / h
        inverse = 1.0 / (h * (1.0 - a * dl) - afb * (fb * slope))
        qq = fb * slope * inverse_h
        cf = h * inverse
        f1 = cf * b
        e2 = b * (fb * qq + dl)
        factors.append(dict(fb=fb, dl=dl, ih=inverse_h, qq=qq, cf=cf, cp=afb * inverse, f1=f1, e1=b * fb * inverse_h, e2=e2))
        slope = d + e2 * f1
    solve(factors, rcv1, 5)
    for c in range(3):
        for R in range(rows_all):
            vs[near_slot(R, 1, c), :] = jnp.where(inside_here, solved(R, c), 0.0)

    particular()
    for c in range(3):
        snd2[pl.ds(c * WINDOW, WINDOW), :] = part[at(0, c), :]
        snd2[pl.ds((3 + c) * WINDOW, WINDOW), :] = part[at(top, c), :]
    sent = gather(snd2, rcv2, 1, pl.ds(0, Q2))
    for copy in sent:
        copy[1].wait_recv()
    copies += sent
    solve(factors, rcv2, 0)
    for c in range(3):
        for R in range(rows_all):
            fin[pl.ds(((2 + c) * rows_all + R) * WINDOW, WINDOW), :] = solved(R, c)
    shared = give(7, 3, 2)
    for copy in shared:
        copy[1].wait_recv()
    copies += shared
    for c in range(3):
        collect(2 + c, lambda x, value: out.__setitem__((c, x), value))
    for condition, copy in copies:
        if condition is None:
            copy.wait_send()
        else:
            pl.when(condition)(copy.wait_send)


def solution(mesh):
    nl, nk = mesh.shape["lat"], mesh.shape["rad"]

    def local(tracer_values, tracer_cell, tracer_count, base_viscosity, velocity, forcing):
        cx, cr, ny = base_viscosity.shape
        slots = tracer_cell.shape[2]
        assert nk == 8 and cx + 2 * HALO == SLOTS and ny == LANES and cr == 12
        total_rows = slots // LANES
        vmem = functools.partial(pltpu.VMEM, dtype=F32)
        field = 2 * cr * SLOTS
        compact = 2 * cr * WINDOW
        spare = 8 * SLOTS
        nc = nk // 2
        scratch = [
            pltpu.SMEM((1, 1, 3), jnp.int32),
            vmem((3 * total_rows, LANES)), pltpu.VMEM((total_rows, LANES), jnp.int32), vmem((cx, cr, LANES)),
            vmem((3, cx, cr, LANES)), vmem((3, cx, cr, LANES)), pltpu.SemaphoreType.DMA((16,)),
            vmem((3 * total_rows, LANES)), vmem((total_rows, LANES)), vmem((total_rows, LANES)),
            vmem((3 * (cr // 2) * SLOTS, 2 * LANES)), vmem((2, 96, LANES)), vmem((72, LANES)), vmem((72, LANES)),
            vmem((2, 96, LANES)), vmem((2, 72, LANES)), vmem((96, LANES)), vmem((3 * (cr // 2) * SLOTS, 2 * LANES)),
            vmem((2, 3, HALO, cr, LANES)), vmem((2, 3, 1, cr, LANES)), vmem((2, HALO, cr, LANES)),
            vmem((3, cx, cr, LANES)), vmem((3, cx, cr, LANES)), vmem((cx, cr, LANES)),
            vmem((3 * field + 2 * spare, LANES)), vmem((3 * field + spare, LANES)), vmem((3 * field + spare, LANES)),
            vmem((field + spare, LANES)), vmem((field, LANES)),
        ]
        scratch += [vmem((compact, LANES))] * 8 + [vmem((3 * compact, LANES)), vmem((2 * field, LANES))]
        scratch += [vmem((Q1, LANES)), vmem((nc, Q1, LANES)), vmem((Q2, LANES)), vmem((nc, Q2, LANES))]
        scratch += [vmem((nc, 3, WINDOW, LANES))] * 2 + [vmem((compact + WINDOW, LANES))]
        scratch += [vmem((5 * compact + spare, LANES)), vmem((5, cr * WINDOW + 8 * WINDOW, LANES))]
        scratch += [pltpu.SemaphoreType.DMA((n,)) for n in (10, 10, 10, 10, 3 * (nc - 1), 3 * (nc - 1))]
        v = pl.BlockSpec(memory_space=pltpu.VMEM)
        h = pl.BlockSpec(memory_space=pltpu.HBM)
        smoothed, composition = pl.pallas_call(
            functools.partial(kernel, nl, nk),
            out_shape=[
                pltpu.VMEM((3, cx, cr, ny), F32),
                pltpu.VMEM((cx * cr * 2, ny), F32),
            ],
            in_specs=[h] * 6,
            out_specs=[v, v],
            scratch_shapes=scratch,
            compiler_params=pltpu.CompilerParams(collective_id=0, has_side_effects=True),
        )(
            tracer_values.reshape(3 * total_rows, LANES),
            tracer_cell.reshape(total_rows, LANES),
            tracer_count,
            base_viscosity,
            velocity,
            forcing,
        )
        return smoothed, jnp.transpose(composition.reshape(cx, cr, 2, ny), (2, 0, 1, 3))

    return jax.shard_map(
        local,
        mesh=mesh,
        in_specs=(
            P("lat", "rad", None, None),
            P("lat", "rad", None),
            P("lat", "rad", None),
            P("lat", "rad", None),
            P(None, "lat", "rad", None),
            P(None, "lat", "rad", None),
        ),
        out_specs=(P(None, "lat", "rad", None), P(None, "lat", "rad", None)),
        check_vma=False,
    )
```

```python
import functools

import jax
import jax.numpy as jnp
from jax import lax
from jax.experimental import pallas as pl
from jax.experimental.pallas import tpu as pltpu
from jax.sharding import PartitionSpec as P

MESH = pl.DeviceIdType.MESH
F32 = jnp.float32
BF16 = jnp.bfloat16

SWEEPS = 2
LATERAL = 0.015625
RADIAL = 32.0
BUOYANCY = 0.1
PRIOR_WEIGHT = 0.5
CONTRAST_BASALT = 2.3
CONTRAST_MELT = 1.5

SLOTS = 16
HALO = 2
LANES = 128
WINDOW = 8
Q1 = 11 * WINDOW
Q2 = 6 * WINDOW


def side_index(cell, first_plane, cr):
    rows = (cell >> 7) - first_plane * cr
    plane = (rows >= cr).astype(jnp.int32)
    radial = rows - cr * plane
    return (plane * 2 + (radial & 1)) * (cr // 2) + (radial >> 1)


def stay_index(cell, cr):
    rows = cell >> 8
    half = cr // 2
    plane = (rows * 43691) >> 18
    return (rows - half * plane) * SLOTS + plane + HALO


def hot_masks(index, tiles):
    base = lax.broadcasted_iota(jnp.int32, (16, LANES), 0).astype(F32)
    return [index == (base + 16.0 * t).astype(BF16) for t in range(tiles)]


def bin_groups(acc, loads, index_a, index_b, first_rows, steps, step_rows, tiles_a, tiles_b, total_rows):
    zero = jnp.zeros((16, LANES), BF16)
    one = jnp.ones((16, LANES), BF16)

    def spread(ref, row):
        return jnp.broadcast_to(ref[pl.ds(row, 1), :], (16, LANES)).astype(BF16)

    def body(step, carry):
        left, right = [], []
        for j in range(step_rows):
            tall, wide = [], []
            for first_row in first_rows:
                row = first_row + step * step_rows + j
                values = [spread(loads, q * total_rows + row) for q in range(3)]
                hot_a = hot_masks(spread(index_a, row), tiles_a)
                hot_b = hot_masks(spread(index_b, row), tiles_b)
                tall += [jnp.where(h, v, zero) for v in values for h in hot_a]
                wide += [jnp.where(h, one, zero) for h in hot_b]
            left.append(jnp.concatenate(tall, 0))
            right.append(jnp.concatenate(wide, 0))
        acc[...] += lax.dot_general(
            jnp.concatenate(left, 1),
            jnp.concatenate(right, 1),
            (((1,), (1,)), ((), ())),
            preferred_element_type=F32,
        )
        return carry

    lax.fori_loop(steps[0], steps[1], body, 0)


def kernel(
    nl, nk, vals_in, cell_in, cnt_in, bv_in, vel_in, frc_in, out, comp,
    cnt, vals, cell, bv, vel, frc, load_sem, loads, index_a, index_b, acc_s, acc_pair, acc_side, edge_lo, edge_hi, got_a, got_b, got_c, got_s,
    hv, hf, hb, pv, pf, pb,
    ext, vs, fs, bs, visc, f_w, f_e, f_s, f_n, up, ip, res0, res1, part, mix,
    snd1, rcv1, snd2, rcv2, flux_lo, flux_hi, share, fin, ret,
    lat_send, lat_recv, chip_send, chip_recv, rad_send, rad_recv,
):
    cx, cr = bv.shape[0], bv.shape[1]
    rows_all = 2 * cr
    half = cr // 2
    total_rows = cell.shape[0]
    rows = total_rows // 3
    nc = nk // 2
    l = lax.axis_index("lat")
    k = lax.axis_index("rad")
    kc = k // 2
    par = lax.rem(k, 2)
    lm = lax.rem(l + nl - 1, nl)
    lp = lax.rem(l + 1, nl)
    odd_below = (lm, 2 * kc + 1)
    even_above = (lp, 2 * kc)
    partner = (l, 2 * kc + 1 - par)
    peers = [(l, 2 * lax.rem(kc + d, nc) + par) for d in range(1, nc)]
    window = par * 6

    has_below = l > 0
    has_above = l < nl - 1
    has_beside = l != par * (nl - 1)

    loading = {4: [pltpu.make_async_copy(cnt_in, cnt, load_sem.at[15])]}
    for g in (0, 2, 1):
        pairs = [(cell_in, cell, g * rows)] + [(vals_in, vals, q * total_rows + g * rows) for q in range(3)]
        loading[g] = [
            pltpu.make_async_copy(src.at[pl.ds(row, rows)], dst.at[pl.ds(row, rows)], load_sem.at[4 * g + n])
            for n, (src, dst, row) in enumerate(pairs)
        ]
    loading[3] = [
        pltpu.make_async_copy(src, dst, load_sem.at[12 + n])
        for n, (src, dst) in enumerate([(bv_in, bv), (vel_in, vel), (frc_in, frc)])
    ]
    for copies in loading.values():
        for copy in copies:
            copy.start()

    barrier = pltpu.get_barrier_semaphore()
    beside = lm + par * (lp - lm)
    for device in [partner] + peers:
        pl.semaphore_signal(barrier, inc=1, device_id=device, device_id_type=MESH)

    @pl.when(has_beside)
    def _():
        for p in range(2):
            pl.semaphore_signal(barrier, inc=1, device_id=(beside, 2 * kc + p), device_id_type=MESH)

    def remote(src, dst, device, send, recv):
        return pltpu.make_async_remote_copy(
            src_ref=src, dst_ref=dst, send_sem=send, recv_sem=recv, device_id=device, device_id_type=MESH
        )

    def to_lat(low, high, dst, n):
        return [
            (has_below, remote(low, dst.at[par], odd_below, lat_send.at[n], lat_recv.at[n + par])),
            (has_above, remote(high, dst.at[par], even_above, lat_send.at[n + 1], lat_recv.at[n + par])),
        ]

    def start(entries):
        for condition, copy in entries:
            if condition is None:
                copy.start()
            else:
                pl.when(condition)(copy.start)

    def from_lat(pairs):
        @pl.when(has_beside)
        def _():
            for dst, n in pairs:
                for p in range(2):
                    remote(dst.at[p], dst.at[p], partner, lat_send.at[n + p], lat_recv.at[n + p]).wait_recv()

    def to_partner(src, dst, n):
        return (None, remote(src, dst, partner, chip_send.at[n], chip_recv.at[n]))

    place = lax.broadcasted_iota(jnp.int32, (rows, LANES), 0) * LANES + lax.broadcasted_iota(
        jnp.int32, (rows, LANES), 1
    )
    step_rows = min(32, rows)
    acc_pair[...] = jnp.zeros_like(acc_pair)
    acc_s[...] = jnp.zeros_like(acc_s)

    def prepare(g):
        for copy in loading[g]:
            copy.wait()
        sl = pl.ds(g * rows, rows)
        weight = jnp.where(place < cnt[0, 0, g], 0.5 + vals[sl, :], 0.0)
        loads[sl, :] = weight
        loads[pl.ds(total_rows + g * rows, rows), :] = weight * vals[pl.ds(total_rows + g * rows, rows), :]
        loads[pl.ds(2 * total_rows + g * rows, rows), :] = weight * vals[pl.ds(2 * total_rows + g * rows, rows), :]
        c = cell[sl, :]
        if g == 1:
            index_a[sl, :] = stay_index(c, cr).astype(F32)
            index_b[sl, :] = (c & 255).astype(F32)
        else:
            index_a[sl, :] = side_index(c, cx - HALO if g == 0 else 0, cr).astype(F32)
            index_b[sl, :] = (c & 127).astype(F32)

    loading[4][0].wait()
    prepare(0)
    prepare(2)
    steps = rows // step_rows

    def bin_pair(begin, end):
        bin_groups(acc_pair, loads, index_a, index_b, (0, 2 * rows), (begin, end), step_rows, 2, 8, total_rows)

    bin_pair(0, steps // 2)

    pl.semaphore_wait(barrier, 1 + len(peers) + jnp.where(has_below, 1, 0) + jnp.where(has_above, 1, 0))
    copies = [to_partner(vel_in, pv, 0), to_partner(frc_in, pf, 1), to_partner(bv_in, pb, 2)]
    copies += to_lat(vel_in.at[:, pl.ds(0, HALO)], vel_in.at[:, pl.ds(cx - HALO, HALO)], hv, 0)
    copies += to_lat(frc_in.at[:, pl.ds(0, 1)], frc_in.at[:, pl.ds(cx - 1, 1)], hf, 2)
    copies += to_lat(bv_in.at[pl.ds(0, HALO)], bv_in.at[pl.ds(cx - HALO, HALO)], hb, 4)
    start(copies)

    bin_pair(steps // 2, steps)
    for g in range(2):
        acc_side[g] = acc_pair[pl.ds(g * 96, 96), pl.ds(g * LANES, LANES)]
    sides = to_lat(acc_side.at[0], acc_side.at[1], got_a, 6) + [to_partner(acc_side.at[1 - par], got_c, 3)]
    start(sides)
    prepare(1)
    long_rows = min(64, rows)
    bin_groups(acc_s, loads, index_a, index_b, (rows,), (0, rows // long_rows), long_rows, 6, 16, total_rows)

    for q in range(3):
        for h in range(2):
            for s in range(HALO):
                row = (q * 4 + s * 2 + h) * half
                lanes = pl.ds(h * LANES, LANES)
                for p in range(half):
                    base = q * half * SLOTS + p * SLOTS
                    edge_lo[pl.ds(row + p, 1), :] = acc_s[pl.ds(base + HALO + s, 1), lanes]
                    edge_hi[pl.ds(row + p, 1), :] = acc_s[pl.ds(base + HALO + cx - HALO + s, 1), lanes]
    late = to_lat(edge_lo, edge_hi, got_b, 8) + [to_partner(acc_s, got_s, 4)]
    start(late)
    copies += sides + late

    field = rows_all * SLOTS

    def put(dst, c, parity, slot, value):
        dst[pl.ds(c * field + parity * cr * SLOTS + slot, cr, stride=SLOTS), :] = value

    near = par * (SLOTS - HALO)

    def kept(value):
        return jnp.where(has_beside, value, 0.0)

    ext[...] = jnp.zeros_like(ext)
    for copy in loading[3]:
        copy.wait()
    for n in range(3):
        copies[n][1].wait_recv()
    for x in range(cx):
        put(bs, 0, par, x + HALO, bv[x])
        put(bs, 0, 1 - par, x + HALO, pb[x])
        for c in range(3):
            put(vs, c, par, x + HALO, vel[c, x])
            put(vs, c, 1 - par, x + HALO, pv[c, x])
            put(fs, c, par, x + HALO, frc[c, x])
            put(fs, c, 1 - par, x + HALO, pf[c, x])
    from_lat([(hv, 0), (hf, 2), (hb, 4)])
    for p in range(2):
        for s in range(HALO):
            put(bs, 0, p, near + s, kept(hb[p, s]))
            for c in range(3):
                put(vs, c, p, near + s, kept(hv[p, c, s]))
        for c in range(3):
            put(fs, c, p, 1 + par * (SLOTS - 3), kept(hf[p, c, 0]))

    def put_edge(ref, block, parity, slot):
        for q in range(3):
            for h in range(2):
                for s in range(HALO):
                    value = ref[pl.ds(q * block + (s * 2 + h) * half, half), :]
                    start = q * field + (parity * cr + h) * SLOTS + slot + s
                    ext[pl.ds(start, half, stride=2 * SLOTS), :] = value

    from_lat([(got_a, 6)])
    for p in range(2):
        got_a[p] = kept(got_a[p])
        put_edge(got_a.at[p], 32, p, HALO + par * (SLOTS - 3 * HALO))
    sides[2][1].wait_recv()
    from_lat([(got_b, 8)])
    for q in range(3):
        theirs, mine = pl.ds(q * 4 * half, 4 * half), pl.ds(q * 32, 4 * half)
        got_b[par, theirs] = kept(got_b[par, theirs]) + acc_side[par, mine]
        got_b[1 - par, theirs] = kept(got_b[1 - par, theirs]) + got_c[mine]
    for p in range(2):
        put_edge(got_b.at[p], 4 * half, p, near)
    late[2][1].wait_recv()

    slot_of = lax.broadcasted_iota(jnp.int32, (SLOTS, LANES), 0)
    lane = lax.broadcasted_iota(jnp.int32, (WINDOW, LANES), 1)
    low = jnp.where(l == 0, HALO, 0)
    high = jnp.where(l == nl - 1, SLOTS - HALO, SLOTS)
    inside = (slot_of >= low) & (slot_of < high)
    slot_here = lax.broadcasted_iota(jnp.int32, (WINDOW, LANES), 0) + window + 1
    inside_here = (slot_here >= low) & (slot_here < high)
    is_south = lane == 0
    is_north = lane == LANES - 1

    def by_slot(R, c=0):
        return pl.ds((c * rows_all + R) * SLOTS, SLOTS)

    def near_slot(R, shift, c=0):
        return pl.ds((c * rows_all + R) * SLOTS + window + shift, WINDOW)

    def at(R, c=0):
        return pl.ds((c * rows_all + R) * WINDOW, WINDOW)

    def south(v):
        return jnp.where(is_south, 0.0, pltpu.roll(v, 1, 1))

    def north(v):
        return jnp.where(is_north, 0.0, pltpu.roll(v, LANES - 1, 1))

    for whose, ref in ((par, acc_s), (1 - par, got_s)):
        for r in range(cr):
            lanes = pl.ds((r & 1) * LANES, LANES)
            sums = []
            for q in range(3):
                more = ext[pl.ds(pl.multiple_of(q * field + (whose * cr + r) * SLOTS, 8), SLOTS), :]
                sums.append(ref[pl.ds((q * half + r // 2) * SLOTS, SLOTS), lanes] + more)
            inverse = 1.0 / (sums[0] + PRIOR_WEIGHT)
            basalt = sums[1] * inverse
            melt = sums[2] * inverse
            here = pl.ds(pl.multiple_of((whose * cr + r) * SLOTS, 8), SLOTS)
            mix[here, :] = basalt
            mix[pl.ds(pl.multiple_of(field + (whose * cr + r) * SLOTS, 8), SLOTS), :] = melt
            heavy = pl.ds(pl.multiple_of(2 * field + (whose * cr + r) * SLOTS, 8), SLOTS)
            fs[heavy, :] = fs[heavy, :] - BUOYANCY * basalt
            visc[here, :] = jnp.where(
                inside, bs[here, :] * jnp.exp(CONTRAST_BASALT * basalt - CONTRAST_MELT * melt), 0.0
            )

    weight_lo = jnp.where(kc == 0, 0.5 * RADIAL, RADIAL)
    weight_hi = jnp.where(kc == nc - 1, 0.5 * RADIAL, RADIAL)
    top = rows_all - 1
    v_at = [visc[near_slot(R, 1), :] for R in range(rows_all)]
    face = [weight_lo * v_at[0]]
    face += [0.5 * RADIAL * (v_at[R - 1] + v_at[R]) for R in range(1, rows_all)]
    face += [weight_hi * v_at[top]]
    face_ref = share
    for R in range(rows_all + 1):
        face_ref[pl.ds(R * WINDOW, WINDOW), :] = face[R]

    def below(R):
        return face_ref[pl.ds(R * WINDOW, WINDOW), :]

    def above(R):
        return below(R + 1)

    def diagonal(R):
        v = visc[near_slot(R, 1), :]
        scale = LATERAL * 0.5
        fw = scale * (v + visc[near_slot(R, 0), :])
        fe = scale * (v + visc[near_slot(R, 2), :])
        fs_, fn = scale * (v + south(v)), scale * (v + north(v))
        f_w[at(R), :] = fw
        f_e[at(R), :] = fe
        f_s[at(R), :] = fs_
        f_n[at(R), :] = fn
        return jnp.where(v > 0.0, fw + fe + fs_ + fn + below(R) + above(R), 1.0)

    u_low = u_high = m_low = m_high = None
    for n in range(cr):
        lo, hi = n, top - n
        p_low, p_high = diagonal(lo), diagonal(hi)
        if n > 0:
            p_low = p_low - below(lo) * u_low
            p_high = p_high - above(hi) * u_high
        i_low, i_high = 1.0 / p_low, 1.0 / p_high
        ip[at(lo), :] = i_low
        ip[at(hi), :] = i_high
        m_low = i_low if n == 0 else below(lo) * m_low * i_low
        m_high = i_high if n == 0 else above(hi) * m_high * i_high
        res0[at(lo), :] = m_low
        res1[at(hi), :] = m_high
        u_low, u_high = above(lo) * i_low, below(hi) * i_high
        up[at(lo), :] = u_low
        up[at(hi), :] = u_high
    middle = 1.0 / (1.0 - u_low * u_high)

    x0, y1 = m_low * middle, m_high * middle
    y0, x1 = u_high * x0, u_low * y1
    for n in range(cr - 1, -1, -1):
        lo, hi = n, top - n
        if n < cr - 1:
            x0 = res0[at(lo), :] + up[at(lo), :] * x0
            x1 = up[at(lo), :] * x1
            y0 = up[at(hi), :] * y0
            y1 = res1[at(hi), :] + up[at(hi), :] * y1
        res0[at(lo), :] = x0
        res1[at(lo), :] = x1
        res0[at(hi), :] = y0
        res1[at(hi), :] = y1

    def right_side(R, c):
        v = vs[near_slot(R, 1, c), :]
        return (
            fs[near_slot(R, 1, c), :]
            + f_w[at(R), :] * vs[near_slot(R, 0, c), :]
            + f_e[at(R), :] * vs[near_slot(R, 2, c), :]
            + f_s[at(R), :] * south(v)
            + f_n[at(R), :] * north(v)
        )

    def particular():
        low_m, high_m = [None] * 3, [None] * 3
        for n in range(cr):
            lo, hi = n, top - n
            for c in range(3):
                a, b = right_side(lo, c), right_side(hi, c)
                if n > 0:
                    a = a + below(lo) * low_m[c]
                    b = b + above(hi) * high_m[c]
                low_m[c] = a * ip[at(lo), :]
                high_m[c] = b * ip[at(hi), :]
                part[at(lo, c), :] = low_m[c]
                part[at(hi, c), :] = high_m[c]
        for c in range(3):
            x = (low_m[c] + u_low * high_m[c]) * middle
            y = high_m[c] + u_high * x
            part[at(cr - 1, c), :] = x
            part[at(cr, c), :] = y
            for n in range(cr - 2, -1, -1):
                lo, hi = n, top - n
                x = part[at(lo, c), :] + up[at(lo), :] * x
                y = part[at(hi, c), :] + up[at(hi), :] * y
                part[at(lo, c), :] = x
                part[at(hi, c), :] = y

    def gather(src, dst, phase, where):
        sent = []
        for d in (2, 1, 3):
            n = phase * (nc - 1) + d - 1
            sent.append((None, remote(src.at[where], dst.at[kc, where], peers[d - 1], rad_send.at[n], rad_recv.at[n])))
        start(sent)
        dst[kc, where] = src[where]
        return sent

    def piece(source, i, number):
        return source[i, pl.ds(number * WINDOW, WINDOW), :]

    def solve(factors, source, first):
        sums = [piece(source, 0, first + 3 + c) for c in range(3)]
        fixed = [[piece(source, 0, first + c) for c in range(3)]]
        olds = [None]
        for i in range(1, nc):
            f = factors[i]
            olds.append([s * f["ih"] for s in sums])
            fixed.append([f["cf"] * piece(source, i, first + c) + f["cp"] * sums[c] for c in range(3)])
            sums = [piece(source, i, first + 3 + c) + f["e1"] * sums[c] + f["e2"] * fixed[i][c] for c in range(3)]
        for c in range(3):
            flux = None
            flux_hi[nc - 1, c] = jnp.zeros((WINDOW, LANES), F32)
            flux_lo[0, c] = jnp.zeros((WINDOW, LANES), F32)
            for i in range(nc - 1, 0, -1):
                f = factors[i]
                first_value = fixed[i][c] if flux is None else fixed[i][c] + f["f1"] * flux
                last_value = olds[i][c] + f["qq"] * first_value
                flux_lo[i, c] = f["fb"] * last_value + f["dl"] * first_value
                flux = f["fb"] * first_value - f["dl"] * last_value
                flux_hi[i - 1, c] = flux

    def solved(R, c):
        return part[at(R, c), :] + res0[at(R), :] * flux_lo[kc, c] + res1[at(R), :] * flux_hi[kc, c]

    for number, value in enumerate([res0[at(0), :], res1[at(0), :], res1[at(top), :], v_at[0], v_at[top]]):
        snd1[pl.ds(number * WINDOW, WINDOW), :] = value
    sent = gather(snd1, rcv1, 2, pl.ds(0, 5 * WINDOW))
    particular()
    for c in range(3):
        snd1[pl.ds((5 + c) * WINDOW, WINDOW), :] = part[at(0, c), :]
        snd1[pl.ds((8 + c) * WINDOW, WINDOW), :] = part[at(top, c), :]
    sent += gather(snd1, rcv1, 0, pl.ds(5 * WINDOW, 6 * WINDOW))
    copies += sent

    for c in range(2):
        for R in range(rows_all):
            fin[pl.ds((c * rows_all + R) * WINDOW, WINDOW), :] = mix[near_slot(R, 1, c), :]

    def give(n, fields, first):
        made = []
        for c in range(fields):
            theirs = pl.ds(pl.multiple_of(((first + c) * rows_all + (1 - par) * cr) * WINDOW, 8), cr * WINDOW)
            made.append(to_partner(fin.at[theirs], ret.at[first + c, pl.ds(0, cr * WINDOW)], n + c))
        start(made)
        return made

    shared = give(5, 2, 0)
    for copy in shared:
        copy[1].wait_recv()
    copies += shared

    def collect(field, store):
        for i in range(1, 1 + cx // 2):
            mine = fin[pl.ds((field * rows_all + par * cr) * WINDOW + i, cr, stride=WINDOW), :]
            theirs = ret[field, pl.ds(i, cr, stride=WINDOW), :]
            store(par * (cx // 2) + i - 1, mine)
            store((1 - par) * (cx // 2) + i - 1, theirs)

    for c in range(2):
        collect(c, lambda x, value: comp.__setitem__((pl.ds(x * 2 * cr + c, cr, stride=2), slice(None)), value))
    for copy in sent:
        copy[1].wait_recv()

    factors = [None]
    slope = piece(rcv1, 0, 2)
    for i in range(1, nc):
        a, b, d, v_first = (piece(rcv1, i, n) for n in (0, 1, 2, 3))
        v_last = piece(rcv1, i - 1, 4)
        fb = 0.5 * RADIAL * (v_last + v_first)
        dl = 0.5 * RADIAL * (v_first - v_last)
        afb = a * fb
        h = 1.0 + slope * dl
        inverse_h = 1.0 / h
        inverse = 1.0 / (h * (1.0 - a * dl) - afb * (fb * slope))
        qq = fb * slope * inverse_h
        cf = h * inverse
        f1 = cf * b
        e2 = b * (fb * qq + dl)
        factors.append(dict(fb=fb, dl=dl, ih=inverse_h, qq=qq, cf=cf, cp=afb * inverse, f1=f1, e1=b * fb * inverse_h, e2=e2))
        slope = d + e2 * f1
    solve(factors, rcv1, 5)
    for c in range(3):
        for R in range(rows_all):
            vs[near_slot(R, 1, c), :] = jnp.where(inside_here, solved(R, c), 0.0)

    particular()
    for c in range(3):
        snd2[pl.ds(c * WINDOW, WINDOW), :] = part[at(0, c), :]
        snd2[pl.ds((3 + c) * WINDOW, WINDOW), :] = part[at(top, c), :]
    sent = gather(snd2, rcv2, 1, pl.ds(0, Q2))
    for copy in sent:
        copy[1].wait_recv()
    copies += sent
    solve(factors, rcv2, 0)
    for c in range(3):
        for R in range(rows_all):
            fin[pl.ds(((2 + c) * rows_all + R) * WINDOW, WINDOW), :] = solved(R, c)
    shared = give(7, 3, 2)
    for copy in shared:
        copy[1].wait_recv()
    copies += shared
    for c in range(3):
        collect(2 + c, lambda x, value: out.__setitem__((c, x), value))
    for condition, copy in copies:
        if condition is None:
            copy.wait_send()
        else:
            pl.when(condition)(copy.wait_send)


def solution(mesh):
    nl, nk = mesh.shape["lat"], mesh.shape["rad"]

    def local(tracer_values, tracer_cell, tracer_count, base_viscosity, velocity, forcing):
        cx, cr, ny = base_viscosity.shape
        slots = tracer_cell.shape[2]
        assert nk == 8 and cx + 2 * HALO == SLOTS and ny == LANES and cr == 12
        total_rows = slots // LANES
        vmem = functools.partial(pltpu.VMEM, dtype=F32)
        field = 2 * cr * SLOTS
        compact = 2 * cr * WINDOW
        spare = 8 * SLOTS
        nc = nk // 2
        scratch = [
            pltpu.SMEM((1, 1, 3), jnp.int32),
            vmem((3 * total_rows, LANES)), pltpu.VMEM((total_rows, LANES), jnp.int32), vmem((cx, cr, LANES)),
            vmem((3, cx, cr, LANES)), vmem((3, cx, cr, LANES)), pltpu.SemaphoreType.DMA((16,)),
            vmem((3 * total_rows, LANES)), vmem((total_rows, LANES)), vmem((total_rows, LANES)),
            vmem((3 * (cr // 2) * SLOTS, 2 * LANES)), vmem((192, 2 * LANES)), vmem((2, 96, LANES)), vmem((72, LANES)), vmem((72, LANES)),
            vmem((2, 96, LANES)), vmem((2, 72, LANES)), vmem((96, LANES)), vmem((3 * (cr // 2) * SLOTS, 2 * LANES)),
            vmem((2, 3, HALO, cr, LANES)), vmem((2, 3, 1, cr, LANES)), vmem((2, HALO, cr, LANES)),
            vmem((3, cx, cr, LANES)), vmem((3, cx, cr, LANES)), vmem((cx, cr, LANES)),
            vmem((3 * field + 2 * spare, LANES)), vmem((3 * field + spare, LANES)), vmem((3 * field + spare, LANES)),
            vmem((field + spare, LANES)), vmem((field, LANES)),
        ]
        scratch += [vmem((compact, LANES))] * 8 + [vmem((3 * compact, LANES)), vmem((2 * field, LANES))]
        scratch += [vmem((Q1, LANES)), vmem((nc, Q1, LANES)), vmem((Q2, LANES)), vmem((nc, Q2, LANES))]
        scratch += [vmem((nc, 3, WINDOW, LANES))] * 2 + [vmem((compact + WINDOW, LANES))]
        scratch += [vmem((5 * compact + spare, LANES)), vmem((5, cr * WINDOW + 8 * WINDOW, LANES))]
        scratch += [pltpu.SemaphoreType.DMA((n,)) for n in (10, 10, 10, 10, 3 * (nc - 1), 3 * (nc - 1))]
        v = pl.BlockSpec(memory_space=pltpu.VMEM)
        h = pl.BlockSpec(memory_space=pltpu.HBM)
        smoothed, composition = pl.pallas_call(
            functools.partial(kernel, nl, nk),
            out_shape=[
                pltpu.VMEM((3, cx, cr, ny), F32),
                pltpu.VMEM((cx * cr * 2, ny), F32),
            ],
            in_specs=[h] * 6,
            out_specs=[v, v],
            scratch_shapes=scratch,
            compiler_params=pltpu.CompilerParams(collective_id=0, has_side_effects=True),
        )(
            tracer_values.reshape(3 * total_rows, LANES),
            tracer_cell.reshape(total_rows, LANES),
            tracer_count,
            base_viscosity,
            velocity,
            forcing,
        )
        return smoothed, jnp.transpose(composition.reshape(cx, cr, 2, ny), (2, 0, 1, 3))

    return jax.shard_map(
        local,
        mesh=mesh,
        in_specs=(
            P("lat", "rad", None, None),
            P("lat", "rad", None),
            P("lat", "rad", None),
            P("lat", "rad", None),
            P(None, "lat", "rad", None),
            P(None, "lat", "rad", None),
        ),
        out_specs=(P(None, "lat", "rad", None), P(None, "lat", "rad", None)),
        check_vma=False,
    )
```
